32 devices in a mesh: fsdp: 8 (over z, x), seq: 4 (over y, core).
Axes of the slice: x: 2, y: 2, z: 4, core: 2. Of those that a mesh axis runs over, the one named last changes fastest.
Arguments:
- tokens: bfloat16 [8192, 768], P(('fsdp', 'seq')), may hold values from -6 to 6
- norm_gains: float32 [2, 2, 768], P(None, None, ('fsdp', 'seq')), may hold values from 0.25 to 1.75
- norm_shifts: float32 [2, 2, 768], P(None, None, ('fsdp', 'seq')), may hold values from -1.5 to 1.5
- w_qkv: float32 [2, 768, 2304], P(None, ('fsdp', 'seq')), may hold values from -0.3125 to 0.3125
- w_out: float32 [2, 768, 768], P(None, ('fsdp', 'seq')), may hold values from -0.875 to 0.875
- w_up: float32 [2, 768, 3072], P(None, ('fsdp', 'seq')), may hold values from -0.21875 to 0.21875
- w_down: float32 [2, 3072, 768], P(None, ('fsdp', 'seq')), may hold values from -0.109375 to 0.109375
- out_grad: bfloat16 [8192, 768], P(('fsdp', 'seq')), may hold values from -6 to 6
- doc_lengths: int32 [8, 8], P('fsdp'), may hold values from 1 to 512, 1024 in all within a row
Outputs:
- outputs: bfloat16 [8192, 768], P(('fsdp', 'seq'))
- grad_tokens: bfloat16 [8192, 768], P(('fsdp', 'seq'))
- grad_norm_gains: float32 [2, 2, 768], P(None, None, ('fsdp', 'seq'))
- grad_attn_shifts: float32 [2, 768], P(None, ('fsdp', 'seq'))
- grad_ffn_shifts: float32 [2, 768], P(None, ('fsdp', 'seq'))
- grad_w_qkv: float32 [2, 768, 2304], P(None, ('fsdp', 'seq'))
- grad_w_out: float32 [2, 768, 768], P(None, ('fsdp', 'seq'))
- grad_w_up: float32 [2, 768, 3072], P(None, ('fsdp', 'seq'))
- grad_w_down: float32 [2, 3072, 768], P(None, ('fsdp', 'seq'))
The draws below stay inside these ranges and needn't reach their ends.
Inputs may be any that keep to these rules, and one draw needn't show every extreme that they name: `doc_lengths`: the lengths of each stream add up to 1024; documents may cross from one device's tokens to the next.
All inputs are finite; a program needn't handle non-finite values.
Results may differ from the reference program's by a relative error of at most 0.023.
The reference program's roundings to bfloat16 on the way count: a program that leaves them out, or rounds other values in their place, can miss the bound.
Values may be sent and summed in bfloat16 or wider, within the bound.
No kernel may reach another device: no remote copies, remote signals or barrier semaphores. Data moves between devices by JAX's collectives and lax.ppermute only.
A program may use at most 256 MiB of HBM per device.

```python
import math
import jax
import jax.numpy as jnp
import numpy as np
from jax import lax

D = 768
H = 12
HD = 64
FF = 3072
LAYERS = 2
DOCS = 8
LEN = 1024
TOKENS = 8192
STREAMS = 8


def levels(stream_key, shape, cuts, smallest, top_value):
    gain, own = 1.0, jax.random.fold_in(stream_key, 6)
    for axis_at, blocks in cuts:
        heights = jnp.exp(jax.random.uniform(jax.random.fold_in(own, axis_at), (blocks,), jnp.float32, smallest / len(cuts), top_value / len(cuts)))
        gain = gain * jnp.repeat(heights, shape[axis_at] // blocks).reshape([-1 if axis == axis_at else 1 for axis in range(len(shape))])
    return gain


def split_up(amount, total, reach, skew):
    portions = [(1 << 20) // math.isqrt(grade ** skew) + 1 for grade in range(2, amount + 1)]
    surplus, given = total - reach - (amount - 1), [1] * (amount - 1)
    while surplus > 0:
        candidates = [i for i in range(amount - 1) if given[i] < reach]
        pool, budget = sum([portions[i] for i in candidates]), surplus
        for i in candidates:
            extra = min(reach - given[i], max(1, budget * portions[i] // pool), surplus)
            given[i] = given[i] + extra
            surplus = surplus - extra
    return np.array([reach] + given)


def uneven_parts(stream_key, count, total, limit, lean):
    if count == 2:
        one = jax.random.randint(stream_key, (), max(1, total - limit), min(limit, total - 1) + 1)
        return jnp.stack([one, total - one])
    sizes = jnp.asarray(split_up(count, total, limit, lean), jnp.int32)
    pairs = (count - 1) // 2
    giver, sink = sizes[1:1 + 2 * pairs:2], sizes[2:2 + 2 * pairs:2]
    margin = jnp.minimum(giver - 1, limit - sink)
    moved = jax.random.randint(jax.random.fold_in(stream_key, 1), (pairs,), 0, 1 << 20) % (margin + 1)
    sizes = sizes.at[1:1 + 2 * pairs:2].set(giver - moved).at[2:2 + 2 * pairs:2].set(sink + moved)
    return sizes[jax.random.permutation(jax.random.fold_in(stream_key, 2), count)]


def centred(rng, extent, scale, limit, pieces=(), held_as=jnp.bfloat16):
    gain = levels(rng, extent, pieces, -0.22, 0.18) if pieces else 1.0
    values = jax.random.normal(rng, extent, jnp.float32) * scale * gain
    return jnp.minimum(jnp.maximum(values, -limit), limit).astype(held_as)


def setup_inputs(seed: int = 0) -> dict:
    keys = jax.random.split(jax.random.key(seed), 10)
    tokens = centred(keys[0], (TOKENS, D), 1.0, 6.0, ((0, 32),))
    norm_gains = jnp.clip(1.0 + 0.15 * jax.random.normal(keys[1], (LAYERS, 2, D), jnp.float32), 0.25, 1.75)
    norm_shifts = centred(keys[2], (LAYERS, 2, D), 0.3, 1.5, ((2, 32),), jnp.float32)
    w_qkv = centred(keys[3], (LAYERS, D, 3 * D), (D // 2) ** -0.5, 0.3125, ((1, 32),), jnp.float32)
    w_out = centred(keys[4], (LAYERS, D, D), (D // 16) ** -0.5, 0.875, ((1, 32),), jnp.float32)
    w_up = centred(keys[5], (LAYERS, D, FF), D ** -0.5, 0.21875, ((1, 32),), jnp.float32)
    w_down = centred(keys[6], (LAYERS, FF, D), FF ** -0.5, 0.109375, ((1, 32),), jnp.float32)
    out_grad = centred(keys[7], (TOKENS, D), 1.0, 6.0, ((0, 32),))
    doc_lengths = jax.vmap(lambda own: uneven_parts(own, DOCS, LEN, LEN // 2, 2))(jax.random.split(keys[8], STREAMS)).reshape((STREAMS, DOCS)).astype(jnp.int32)
    return {"tokens": tokens, "norm_gains": norm_gains, "norm_shifts": norm_shifts, "w_qkv": w_qkv, "w_out": w_out, "w_up": w_up, "w_down": w_down, "out_grad": out_grad, "doc_lengths": doc_lengths}


@jax.custom_vjp
def low(v):
    return lax.optimization_barrier(v.astype(jnp.bfloat16)).astype(jnp.float32)

@jax.custom_vjp
def low_back(v):
    return v

def low_keep(v):
    return (low(v), None)

def low_pass(kept, grad):
    return (grad,)

def back_keep(v):
    return (v, None)

def back_low(kept, grad):
    return (low(grad),)
low.defvjp(low_keep, low_pass)
low_back.defvjp(back_keep, back_low)
NORM_EPS = 1e-05
BRANCH_SCALE = 0.7071067811865476
MASKED = -1e+30
HIGHEST = lax.Precision.HIGHEST

def layer_norm(values, gain_row, shift_row):
    center = values - lax.optimization_barrier(jnp.mean(values, axis=-1, keepdims=True))
    spread = lax.optimization_barrier(jnp.mean(center * center, axis=-1, keepdims=True))
    return center * lax.rsqrt(spread + NORM_EPS) * gain_row + shift_row

def gelu_tanh(values):
    return 0.5 * values * (1.0 + jnp.tanh(0.7978845608028654 * (values + 0.044715 * values * values * values)))

def product(left_side, right_side):
    return jnp.dot(left_side, right_side, precision=HIGHEST, preferred_element_type=jnp.float32)

def attention(queries, keys_all, values_all, segment):
    length = queries.shape[0]
    block_rows = min(512, length)
    score_scale = HD ** (-0.5)
    positions = jnp.arange(length, dtype=jnp.int32)

    def one_block(block_index):
        row_start = (block_index * block_rows).astype(jnp.int32)
        query_block = lax.dynamic_slice_in_dim(queries, row_start, block_rows, 0)
        scores = jnp.einsum('qhd,khd->hqk', query_block, keys_all, precision=HIGHEST) * score_scale
        scores = low_back(scores)
        query_pos = row_start + jnp.arange(block_rows, dtype=jnp.int32)
        query_seg = lax.dynamic_slice_in_dim(segment, row_start, block_rows, 0)
        allowed = (query_pos[:, None] >= positions[None, :]) & (query_seg[:, None] == segment[None, :])
        masked = jnp.where(allowed[None], scores, MASKED)
        shifted = masked - lax.optimization_barrier(jnp.max(masked, axis=2, keepdims=True))
        exponent = jnp.exp(shifted)
        denominator = lax.optimization_barrier(jnp.sum(exponent, axis=2, keepdims=True))
        probs_low = low(exponent / denominator)
        attended_block = jnp.einsum('hqk,khd->qhd', probs_low, values_all, precision=HIGHEST)
        return attended_block.reshape(block_rows, H * HD)
    blocks = lax.map(jax.checkpoint(one_block), jnp.arange(length // block_rows, dtype=jnp.int32))
    return blocks.reshape(length, H * HD)

def stream_forward(hidden, norm_gains, norm_shifts, w_qkv, w_out, w_up, w_down, segment):
    length = hidden.shape[0]
    for layer_index in range(LAYERS):
        gain_rows = low(norm_gains[layer_index])
        shift_rows = low(norm_shifts[layer_index])
        normed_a = low(layer_norm(hidden, gain_rows[0], shift_rows[0]))
        mixed_rows = low(low_back(product(normed_a, low(w_qkv[layer_index]))))
        mixed_rows = mixed_rows.reshape(length, 3, H, HD)
        attended = attention(mixed_rows[:, 0], mixed_rows[:, 1], mixed_rows[:, 2], segment)
        attended = low(low_back(attended))
        branch = low_back(product(attended, low(w_out[layer_index])))
        hidden = hidden + BRANCH_SCALE * branch
        normed_b = low(layer_norm(hidden, gain_rows[1], shift_rows[1]))
        upper_rows = low_back(product(normed_b, low(w_up[layer_index])))
        active = low(gelu_tanh(upper_rows))
        branch = low_back(product(active, low(w_down[layer_index])))
        hidden = hidden + BRANCH_SCALE * branch
    return hidden

def reference(tokens, norm_gains, norm_shifts, w_qkv, w_out, w_up, w_down, out_grad, doc_lengths):
    streams = doc_lengths.shape[0]
    length = tokens.shape[0] // streams
    params = (norm_gains, norm_shifts, w_qkv, w_out, w_up, w_down)

    def per_stream(totals_sum, stream_item):
        stream_rows, stream_cot, lengths = stream_item
        starts = (jnp.cumsum(lengths) - lengths).astype(jnp.int32)
        positions = jnp.arange(length, dtype=jnp.int32)
        segment = lax.optimization_barrier(jnp.sum((positions[:, None] >= starts[None, :]).astype(jnp.int32), axis=1)).astype(jnp.int32)

        def forward(hidden, gains_in, shifts_in, qkv_in, out_in, up_in, down_in):
            return stream_forward(hidden, gains_in, shifts_in, qkv_in, out_in, up_in, down_in, segment)
        result, pull_back = jax.vjp(forward, stream_rows.astype(jnp.float32), norm_gains, norm_shifts, w_qkv, w_out, w_up, w_down)
        stream_grads = pull_back(stream_cot.astype(jnp.float32))
        new_totals = tuple((total_part + grad_part for total_part, grad_part in zip(totals_sum, stream_grads[1:])))
        return (new_totals, (result.astype(jnp.bfloat16), stream_grads[0].astype(jnp.bfloat16)))
    zero_grads = tuple((jnp.zeros_like(member) for member in params))
    totals_sum, (results, input_grads) = lax.scan(per_stream, zero_grads, (tokens.reshape(streams, length, D), out_grad.reshape(streams, length, D), doc_lengths))
    return (results.reshape(streams * length, D), input_grads.reshape(streams * length, D), totals_sum[0], totals_sum[1][:, 0], totals_sum[1][:, 1], totals_sum[2], totals_sum[3], totals_sum[4], totals_sum[5])
```

```python
import jax
import jax.numpy as jnp
from jax import lax
from jax.experimental import pallas as pl
from jax.experimental.pallas import tpu as pltpu
from jax.sharding import PartitionSpec as P

H = 12
HD = 64
LAYERS = 2
MAX_DOC = 512

NORM_EPS = 1e-05
BRANCH_SCALE = 0.7071067811865476
MASKED = -1e30
BF = jnp.bfloat16
F32 = jnp.float32
BOTH = ("fsdp", "seq")

RING_NEXT = (1, 3, 0, 2)
RING_PREV = (2, 0, 3, 1)


def pick(table, index):
    return jnp.array(table, jnp.int32)[index]


def swap_seq(values, bit):
    return lax.ppermute(values, "seq", [(s, s ^ bit) for s in range(4)])


def by_bit(bit, own, other):
    zero = bit == 0
    return jnp.where(zero, own, other), jnp.where(zero, other, own)


def gather_seq(rows):
    place = lax.axis_index("seq")
    far = swap_seq(rows, 2)
    pair = jnp.stack(by_bit(place // 2, rows, far))
    near = swap_seq(pair, 1)
    return jnp.stack(by_bit(place % 2, pair, near), axis=1).reshape(-1, rows.shape[-1])


def scatter_seq(partial):
    place = lax.axis_index("seq")
    y_bit, c_bit = place // 2, place % 2
    width = partial.shape[-1]
    parts = partial.reshape(2, 2, -1, width)
    sent = lax.dynamic_index_in_dim(parts, 1 - c_bit, 1, keepdims=False).astype(BF)
    kept = lax.dynamic_index_in_dim(parts, c_bit, 1, keepdims=False).astype(F32)
    half = kept + swap_seq(sent, 1).astype(F32)
    sent = lax.dynamic_index_in_dim(half, 1 - y_bit, 0, keepdims=False).astype(BF)
    kept = lax.dynamic_index_in_dim(half, y_bit, 0, keepdims=False)
    return kept + swap_seq(sent, 2).astype(F32)


def exchange_seq(parts):
    place = lax.axis_index("seq")
    y_bit, c_bit = place // 2, place % 2
    grid = parts.reshape((2, 2) + parts.shape[1:])
    kept, sent = by_bit(c_bit, grid[:, 0], grid[:, 1])
    half = jnp.stack(by_bit(c_bit, kept, swap_seq(sent, 1)), axis=1)
    kept, sent = by_bit(y_bit, half[0], half[1])
    return jnp.stack(by_bit(y_bit, kept, swap_seq(sent, 2))).reshape(parts.shape)


def gather_fsdp(block):
    count = lax.axis_size("fsdp")
    if count != 8:
        return lax.all_gather(block, "fsdp", axis=0, tiled=False)
    place = lax.axis_index("fsdp")
    line, side = place // 2, place % 2
    ring = [(f, 2 * RING_NEXT[f // 2] + f % 2) for f in range(8)]
    gathered = jnp.zeros((4,) + block.shape, block.dtype)
    source = line
    for step in range(4):
        gathered = lax.dynamic_update_index_in_dim(gathered, block, source, 0)
        if step < 3:
            block = lax.ppermute(block, "fsdp", ring)
            source = pick(RING_PREV, source)
    other = lax.ppermute(gathered, "fsdp", [(f, f ^ 1) for f in range(8)])
    return jnp.stack(by_bit(side, gathered, other), axis=1).reshape((8,) + block.shape)


def scatter_fsdp(blocks):
    count = lax.axis_size("fsdp")
    if count != 8:
        return lax.psum_scatter(blocks.astype(BF), "fsdp", scatter_dimension=0, tiled=False).astype(F32)
    place = lax.axis_index("fsdp")
    line, side = place // 2, place % 2
    ring = [(f, 2 * RING_NEXT[f // 2] + f % 2) for f in range(8)]
    grid = blocks.reshape((4, 2) + blocks.shape[1:])
    sent = lax.dynamic_index_in_dim(grid, 1 - side, 1, keepdims=False).astype(BF)
    kept = lax.dynamic_index_in_dim(grid, side, 1, keepdims=False).astype(F32)
    kept = kept + lax.ppermute(sent, "fsdp", [(f, f ^ 1) for f in range(8)]).astype(F32)
    owner = pick(RING_PREV, line)
    running = lax.dynamic_index_in_dim(kept, owner, 0, keepdims=False)
    for _ in range(3):
        running = lax.ppermute(running.astype(BF), "fsdp", ring).astype(F32)
        owner = pick(RING_PREV, owner)
        running = running + lax.dynamic_index_in_dim(kept, owner, 0, keepdims=False)
    return running


def turn(rows):
    moves = []
    for f in range(8):
        for s in range(4):
            moves.append((f * 4 + s, (2 * s + f % 2) * 4 + f // 2))
    return lax.ppermute(rows, BOTH, moves)


ROWS = 256


def allowed_pairs(first_ref, row_start, key_start, width):
    key_pos = key_start + lax.broadcasted_iota(jnp.int32, (ROWS, width), 1)
    query_pos = row_start + lax.broadcasted_iota(jnp.int32, (ROWS, width), 0)
    first = first_ref[pl.ds(row_start, ROWS), :]
    return (key_pos <= query_pos) & (key_pos >= first)


def key_window(row_start):
    key_start = max(0, row_start - (MAX_DOC + ROWS - 1) // ROWS * ROWS)
    return key_start, row_start + ROWS - key_start


def dot_t(left, right):
    return lax.dot_general(left, right, (((1,), (1,)), ((), ())), preferred_element_type=F32)


def t_dot(left, right):
    return lax.dot_general(left, right, (((0,), (0,)), ((), ())), preferred_element_type=F32)


def attend_kernel(first_ref, mixed_ref, out_ref, total_ref):
    length, group = out_ref.shape
    heads = group // HD
    scale = HD ** (-0.5)
    for row_start in range(0, length, ROWS):
        key_start, width = key_window(row_start)
        allowed = allowed_pairs(first_ref, row_start, key_start, width)
        outs = []
        totals = []
        for head in range(heads):
            at = head * HD
            query = mixed_ref[pl.ds(row_start, ROWS), pl.ds(at, HD)]
            keys = mixed_ref[pl.ds(key_start, width), pl.ds(group + at, HD)]
            values = mixed_ref[pl.ds(key_start, width), pl.ds(2 * group + at, HD)]
            scores = jnp.where(allowed, dot_t(query, keys) * scale, MASKED)
            top = jnp.max(scores, axis=1, keepdims=True)
            weights = jnp.exp(scores - top)
            total = jnp.sum(weights, axis=1, keepdims=True)
            low = (weights * (1.0 / total)).astype(BF)
            outs.append(jnp.dot(low, values, preferred_element_type=F32))
            totals.append(top + jnp.log(total))
        out_ref[pl.ds(row_start, ROWS), :] = jnp.concatenate(outs, axis=1).astype(BF)
        total_ref[pl.ds(row_start, ROWS), :] = jnp.concatenate(totals, axis=1)


def attend(first, mixed):
    length, wide = mixed.shape
    group = wide // 3
    return pl.pallas_call(
        attend_kernel,
        out_shape=(
            jax.ShapeDtypeStruct((length, group), BF),
            jax.ShapeDtypeStruct((length, group // HD), F32),
        ),
        compiler_params=pltpu.CompilerParams(vmem_limit_bytes=48 << 20),
        name="attend",
    )(first, mixed)


def attend_back_kernel(first_ref, mixed_ref, total_ref, cot_ref, out_ref, key_acc, value_acc):
    length, group = cot_ref.shape
    heads = group // HD
    scale = HD ** (-0.5)
    key_acc[...] = jnp.zeros_like(key_acc)
    value_acc[...] = jnp.zeros_like(value_acc)
    for row_start in range(0, length, ROWS):
        key_start, width = key_window(row_start)
        allowed = allowed_pairs(first_ref, row_start, key_start, width)
        query_grads = []
        key_grads = []
        value_grads = []
        for head in range(heads):
            at = head * HD
            query = mixed_ref[pl.ds(row_start, ROWS), pl.ds(at, HD)]
            keys = mixed_ref[pl.ds(key_start, width), pl.ds(group + at, HD)]
            values = mixed_ref[pl.ds(key_start, width), pl.ds(2 * group + at, HD)]
            cot = cot_ref[pl.ds(row_start, ROWS), pl.ds(at, HD)]
            total = total_ref[pl.ds(row_start, ROWS), pl.ds(head, 1)]
            scores = jnp.where(allowed, dot_t(query, keys) * scale - total, MASKED)
            probs = jnp.exp(scores)
            prob_cot = dot_t(cot, values)
            delta = jnp.sum(probs * prob_cot, axis=1, keepdims=True)
            score_cot = (probs * (prob_cot - delta)).astype(BF)
            query_grads.append(jnp.dot(score_cot, keys, preferred_element_type=F32) * scale)
            key_grads.append(t_dot(score_cot, query) * scale)
            value_grads.append(t_dot(probs.astype(BF), cot))
        out_ref[pl.ds(row_start, ROWS), pl.ds(0, group)] = jnp.concatenate(query_grads, axis=1).astype(BF)
        window = pl.ds(key_start, width)
        key_acc[window, :] += jnp.concatenate(key_grads, axis=1)
        value_acc[window, :] += jnp.concatenate(value_grads, axis=1)
    out_ref[:, pl.ds(group, group)] = key_acc[...].astype(BF)
    out_ref[:, pl.ds(2 * group, group)] = value_acc[...].astype(BF)


def attend_back(first, mixed, totals, cot):
    length, wide = mixed.shape
    group = wide // 3
    return pl.pallas_call(
        attend_back_kernel,
        out_shape=jax.ShapeDtypeStruct((length, wide), BF),
        scratch_shapes=[pltpu.VMEM((length, group), F32), pltpu.VMEM((length, group), F32)],
        compiler_params=pltpu.CompilerParams(vmem_limit_bytes=48 << 20),
        name="attend_back",
    )(first, mixed, totals, cot)


def norm_parts(values):
    center = values - jnp.mean(values, axis=-1, keepdims=True)
    inverse = lax.rsqrt(jnp.mean(center * center, axis=-1, keepdims=True) + NORM_EPS)
    return center * inverse, inverse


def norm_back(unit, inverse, gain, cot):
    scaled = cot * gain
    inner = scaled - jnp.mean(scaled, axis=-1, keepdims=True)
    inner = inner - unit * jnp.mean(scaled * unit, axis=-1, keepdims=True)
    return inner * inverse, jnp.sum(cot * unit, axis=0), jnp.sum(cot, axis=0)


def gelu_tanh(values):
    return 0.5 * values * (1.0 + jnp.tanh(0.7978845608028654 * (values + 0.044715 * values * values * values)))


def gelu_slope(values):
    square = values * values
    bent = jnp.tanh(0.7978845608028654 * (values + 0.044715 * values * square))
    inner = 0.7978845608028654 * (1.0 + 3.0 * 0.044715 * square)
    return 0.5 * (1.0 + bent) + 0.5 * values * (1.0 - bent * bent) * inner


def mul(left, right):
    return jnp.dot(left, right, preferred_element_type=F32)


def shards(tokens, norm_gains, norm_shifts, w_qkv, w_out, w_up, w_down, out_grad, doc_lengths):
    tok_rows, width = tokens.shape
    fsdp, seq = lax.axis_size("fsdp"), lax.axis_size("seq")
    ruled = fsdp == 8
    length = tok_rows * seq
    group = (H // seq) * HD
    piece = w_qkv.shape[1]
    inner = w_up.shape[2] // seq
    place = lax.axis_index("seq")

    ends = jnp.cumsum(doc_lengths[0])
    starts = ends - doc_lengths[0]
    positions = lax.iota(jnp.int32, length)
    first = jnp.max(jnp.where(positions[:, None] >= starts[None, :], starts[None, :], 0), axis=1, keepdims=True)

    def column_parts(layer):
        qkv = w_qkv[layer].astype(BF).reshape(piece, 3, seq, group).transpose(2, 0, 1, 3)
        up = w_up[layer].astype(BF).reshape(piece, seq, inner).transpose(1, 0, 2)
        return qkv.reshape(seq, piece, 3 * group), up

    def pad_cols(values, cols):
        return jnp.pad(values, [(0, 0)] * (values.ndim - 1) + [(0, cols - values.shape[-1])])

    norms = jnp.stack([norm_gains, norm_shifts]).astype(BF).reshape(1, 1, 8 * piece)
    qkv_parts = [None, None]
    up_parts = [None, None]
    for layer in range(LAYERS):
        qkv_parts[layer], up_parts[layer] = column_parts(layer)
    sent = jnp.concatenate([qkv_parts[0], jnp.broadcast_to(pad_cols(norms, 3 * group), (seq, 8, 3 * group))], axis=1)
    early = exchange_seq(sent).reshape(seq, piece + 8, 3 * group)
    early = gather_fsdp(early)
    qkv_low = [early[:, :, :piece].reshape(width, 3 * group), None]
    norm_low = early[:, :, piece, : 8 * piece].reshape(fsdp * seq, 2, LAYERS, 2, piece)
    norm_low = norm_low.transpose(1, 2, 3, 0, 4).reshape(2, LAYERS, 2, width).astype(F32)
    gains, shifts = norm_low[0], norm_low[1]

    later = jnp.concatenate([up_parts[0], pad_cols(qkv_parts[1], inner), up_parts[1]], axis=1)
    later = exchange_seq(later)
    rows_of = piece + w_down.shape[1]
    if ruled:
        turned = jnp.concatenate([w_out[0], w_down[0], w_out[1], w_down[1]]).astype(BF)
        turned = turn(turned)
        turned = [turned[:rows_of], turned[rows_of:]]

        def unturn(gathered):
            rest = gathered.shape[1:]
            return gathered.reshape((4, 2) + rest).transpose((1, 0) + tuple(range(2, 2 + len(rest)))).reshape(-1, rest[-1])

    out_low = [None, None]
    up_low = [None, None]
    down_low = [None, None]
    for layer in range(LAYERS):
        if layer == 0:
            cols = later[:, :piece].reshape(seq * piece, inner)
        else:
            cols = later[:, piece:].reshape(seq * 2 * piece, inner)
        taken = cols.shape[0]
        if ruled:
            cols = jnp.concatenate([cols, turned[layer]])
        cols = gather_fsdp(cols)
        if layer == 0:
            up_low[0] = cols[:, :taken].reshape(width, inner)
        else:
            both = cols[:, :taken].reshape(fsdp, seq, 2, piece, inner)
            qkv_low[1] = both[:, :, 0, :, : 3 * group].reshape(width, 3 * group)
            up_low[1] = both[:, :, 1].reshape(width, inner)
        if ruled:
            rows = cols[:, taken:]
            out_low[layer] = unturn(rows[:, :piece])
            down_low[layer] = unturn(rows[:, piece:])
        else:
            whole = lax.all_gather(w_out[layer].astype(BF), BOTH, axis=0, tiled=True)
            out_low[layer] = lax.dynamic_slice_in_dim(whole, place * group, group, 0)
            whole = lax.all_gather(w_down[layer].astype(BF), BOTH, axis=0, tiled=True)
            down_low[layer] = lax.dynamic_slice_in_dim(whole, place * inner, inner, 0)

    hidden = tokens.astype(F32)
    saved = []
    for layer in range(LAYERS):
        unit_a, inverse_a = norm_parts(hidden)
        normed_a = gather_seq((unit_a * gains[layer, 0] + shifts[layer, 0]).astype(BF))
        mixed = mul(normed_a, qkv_low[layer]).astype(BF)
        attended, totals = attend(first, mixed)
        hidden = hidden + BRANCH_SCALE * scatter_seq(mul(attended, out_low[layer]))
        unit_b, inverse_b = norm_parts(hidden)
        normed_b = gather_seq((unit_b * gains[layer, 1] + shifts[layer, 1]).astype(BF))
        upper = mul(normed_b, up_low[layer])
        active = gelu_tanh(upper).astype(BF)
        hidden = hidden + BRANCH_SCALE * scatter_seq(mul(active, down_low[layer]))
        saved.append((unit_a, inverse_a, normed_a, mixed, attended, totals, unit_b, inverse_b, normed_b, upper, active))
    outputs = hidden.astype(BF)

    cot = out_grad.astype(F32)
    norm_sums = []
    qkv_grads = [None, None]
    out_grads = [None, None]
    up_grads = [None, None]
    down_grads = [None, None]

    def cols_blocks(grad):
        return grad.reshape(fsdp, seq * piece, -1)

    def rows_blocks(grad):
        if not ruled:
            return None
        each = grad.shape[0] // 8
        return grad.reshape(2, 4, each, -1).transpose(1, 0, 2, 3).reshape(8, each, -1)

    def rows_whole(grad):
        spread = jnp.zeros((seq,) + grad.shape, BF)
        spread = lax.dynamic_update_index_in_dim(spread, grad.astype(BF), place, 0).reshape(seq * grad.shape[0], -1)
        return lax.psum_scatter(spread, BOTH, scatter_dimension=0, tiled=True).astype(F32)

    def reduce_blocks(parts):
        joined = scatter_fsdp(jnp.concatenate(parts, axis=1))
        taken = []
        at = 0
        for part in parts:
            taken.append(joined[at : at + part.shape[1]])
            at += part.shape[1]
        return taken

    pending = {}
    for layer in reversed(range(LAYERS)):
        unit_a, inverse_a, normed_a, mixed, attended, totals, unit_b, inverse_b, normed_b, upper, active = saved[layer]
        down_cot = gather_seq((BRANCH_SCALE * cot).astype(BF))
        grad_down = t_dot(active, down_cot)
        upper_cot = (gelu_slope(upper) * dot_t(down_cot, down_low[layer])).astype(BF)
        grad_up = t_dot(normed_b, upper_cot)
        second_cot = scatter_seq(dot_t(upper_cot, up_low[layer]))
        back, gain_sum_b, shift_sum_b = norm_back(unit_b, inverse_b, gains[layer, 1], second_cot)
        cot = cot + back
        attn_cot = gather_seq((BRANCH_SCALE * cot).astype(BF))
        grad_out = t_dot(attended, attn_cot)
        attended_cot = dot_t(attn_cot, out_low[layer]).astype(BF)
        mixed_cot = attend_back(first, mixed, totals, attended_cot)
        grad_qkv = t_dot(normed_a, mixed_cot)
        normed_cot = scatter_seq(dot_t(mixed_cot, qkv_low[layer]))
        back, gain_sum_a, shift_sum_a = norm_back(unit_a, inverse_a, gains[layer, 0], normed_cot)
        cot = cot + back
        norm_sums.append(jnp.stack([gain_sum_a, gain_sum_b, shift_sum_a, shift_sum_b]))
        pending[layer] = (grad_qkv, grad_out, grad_up, grad_down)

    turned_back = {}
    column_back = {}
    qkv1, out1, up1, down1 = pending[1]
    qkv0, out0, up0, down0 = pending[0]
    if ruled:
        column_back["up1"], down1_t, out1_t = reduce_blocks([cols_blocks(up1), rows_blocks(down1), rows_blocks(out1)])
        qkv1_p, column_back["up0"], down0_t = reduce_blocks(
            [pad_cols(cols_blocks(qkv1), inner), cols_blocks(up0), rows_blocks(down0)]
        )
        column_back["qkv1"] = qkv1_p[:, : 3 * group]
        (out0_t,) = reduce_blocks([rows_blocks(out0)])
        (column_back["qkv0"],) = reduce_blocks([cols_blocks(qkv0)])
        back = turn(jnp.concatenate([out1_t, down1_t]).astype(BF)).astype(F32)
        out_grads[1], down_grads[1] = back[:piece], back[piece:]
        back = turn(down0_t.astype(BF)).astype(F32)
        down_grads[0] = back
        out_grads[0] = turn(out0_t.astype(BF)).astype(F32)
    else:
        for name, grad in (("up1", up1), ("qkv1", qkv1), ("up0", up0), ("qkv0", qkv0)):
            (column_back[name],) = reduce_blocks([cols_blocks(grad)])
        out_grads = [rows_whole(out0), rows_whole(out1)]
        down_grads = [rows_whole(down0), rows_whole(down1)]

    def column_home(grad):
        return exchange_seq(grad.astype(BF).reshape(seq, piece, -1)).astype(F32)

    for layer in range(LAYERS):
        up_grads[layer] = column_home(column_back["up%d" % layer]).transpose(1, 0, 2).reshape(piece, -1)
        qkv_home = column_home(column_back["qkv%d" % layer]).reshape(seq, piece, 3, group)
        qkv_grads[layer] = qkv_home.transpose(1, 2, 0, 3).reshape(piece, -1)

    sums = jnp.concatenate(norm_sums[::-1])
    if ruled:
        for bit in (1, 2):
            sums = sums + swap_seq(sums, bit)
        for bit in (1, 2, 4):
            sums = sums + lax.ppermute(sums, "fsdp", [(f, f ^ bit) for f in range(8)])
    else:
        sums = lax.psum(sums, BOTH)
    whose = lax.axis_index("fsdp") * seq + place
    sums = lax.dynamic_slice_in_dim(sums, whose * piece, piece, 1).reshape(LAYERS, 4, piece)
    return (
        outputs,
        cot.astype(BF),
        sums[:, :2],
        sums[:, 2],
        sums[:, 3],
        jnp.stack(qkv_grads),
        jnp.stack(out_grads),
        jnp.stack(up_grads),
        jnp.stack(down_grads),
    )


def solution(mesh):
    rows = P(BOTH, None)
    thirds = P(None, None, BOTH)
    middle = P(None, BOTH, None)
    return jax.shard_map(
        shards,
        mesh=mesh,
        in_specs=(rows, thirds, thirds, middle, middle, middle, middle, rows, P("fsdp", None)),
        out_specs=(rows, rows, thirds, P(None, BOTH), P(None, BOTH), middle, middle, middle, middle),
        check_vma=False,
    )
```

```python
import jax
import jax.numpy as jnp
from jax import lax
from jax.experimental import pallas as pl
from jax.experimental.pallas import tpu as pltpu
from jax.sharding import PartitionSpec as P

H = 12
HD = 64
LAYERS = 2
MAX_DOC = 512

NORM_EPS = 1e-05
BRANCH_SCALE = 0.7071067811865476
MASKED = -1e30
BF = jnp.bfloat16
F32 = jnp.float32
BOTH = ("fsdp", "seq")

RING_NEXT = (1, 3, 0, 2)


def ring_behind(line, steps):
    at = ((line ^ (line >> 1)) - steps) & 3
    return at ^ (at >> 1)


def after(value, *others):
    return lax.optimization_barrier((value,) + others)[0] if others else value


def swap_seq(values, bit):
    return lax.ppermute(values, "seq", [(s, s ^ bit) for s in range(4)])


def by_bit(bit, own, other):
    zero = bit == 0
    return jnp.where(zero, own, other), jnp.where(zero, other, own)


def gather_seq(rows, work=None):
    place = lax.axis_index("seq")
    far = swap_seq(rows, 2)
    if work is not None:
        far = after(far, *work(rows))
    pair = jnp.stack(by_bit(place // 2, rows, far))
    near = swap_seq(pair, 1)
    return jnp.stack(by_bit(place % 2, pair, near), axis=1).reshape(-1, rows.shape[-1])


def scatter_seq(partial, work=None):
    place = lax.axis_index("seq")
    y_bit, c_bit = place // 2, place % 2
    width = partial.shape[-1]
    parts = partial.reshape(2, 2, -1, width)
    sent = lax.dynamic_index_in_dim(parts, 1 - c_bit, 1, keepdims=False).astype(BF)
    kept = lax.dynamic_index_in_dim(parts, c_bit, 1, keepdims=False).astype(F32)
    half = kept + swap_seq(sent, 1).astype(F32)
    sent = lax.dynamic_index_in_dim(half, 1 - y_bit, 0, keepdims=False).astype(BF)
    kept = lax.dynamic_index_in_dim(half, y_bit, 0, keepdims=False)
    got = swap_seq(sent, 2)
    if work is not None:
        got = after(got, *work(sent))
    return kept + got.astype(F32)


def exchange_seq(parts):
    place = lax.axis_index("seq")
    y_bit, c_bit = place // 2, place % 2
    grid = parts.reshape((2, 2) + parts.shape[1:])
    kept, sent = by_bit(c_bit, grid[:, 0], grid[:, 1])
    half = jnp.stack(by_bit(c_bit, kept, swap_seq(sent, 1)), axis=1)
    kept, sent = by_bit(y_bit, half[0], half[1])
    return jnp.stack(by_bit(y_bit, kept, swap_seq(sent, 2))).reshape(parts.shape)


def over_line(block):
    return lax.ppermute(block, "fsdp", [(f, 2 * RING_NEXT[f // 2] + f % 2) for f in range(8)])


def over_side(block):
    return lax.ppermute(block, "fsdp", [(f, f ^ 1) for f in range(8)])


def owner(steps, other=0):
    place = lax.axis_index("fsdp")
    return 2 * ring_behind(place // 2, steps) + (place % 2 ^ other)


class Gather:
    def __init__(self, block):
        self.got = block
        self.step = 0
        self.result = jnp.zeros((8,) + block.shape, block.dtype)

    def put(self, block, place):
        self.result = lax.dynamic_update_index_in_dim(self.result, block, place, 0)

    def advance(self, *gates):
        moved = []
        if self.step > 0:
            self.put(after(self.side, *gates), owner(self.step - 1, 1))
        if self.step < 4:
            block = after(self.got, *gates)
            moved.append(block)
            if self.step < 3:
                self.got = over_line(block)
            self.side = over_side(block)
            self.put(block, owner(self.step))
        self.step += 1
        return moved


class Reduce:
    def __init__(self, blocks):
        self.blocks = blocks
        self.step = 0

    def take(self, place):
        return lax.dynamic_index_in_dim(self.blocks, place, 0, keepdims=False)

    def advance(self, *gates):
        moved = []
        if self.step > 0:
            total = self.take(owner(self.step)).astype(F32) + after(self.side, *gates).astype(F32)
            if self.step > 1:
                total = total + after(self.got, *gates).astype(F32)
            if self.step < 4:
                total = total.astype(BF)
                self.got = over_line(total)
            self.result = total
            moved.append(total)
        if self.step < 4:
            block = self.take(owner(self.step + 1, 1))
            if gates:
                block = after(block, *gates)
            self.side = over_side(block)
            moved.append(block)
        self.step += 1
        return moved


def turn(rows):
    moves = []
    for f in range(8):
        for s in range(4):
            moves.append((f * 4 + s, (2 * s + f % 2) * 4 + f // 2))
    return lax.ppermute(rows, BOTH, moves)


ROWS = 256


def allowed_pairs(first_ref, row_start, key_start, width):
    key_pos = key_start + lax.broadcasted_iota(jnp.int32, (ROWS, width), 1)
    query_pos = row_start + lax.broadcasted_iota(jnp.int32, (ROWS, width), 0)
    first = first_ref[pl.ds(row_start, ROWS), :]
    return (key_pos <= query_pos) & (key_pos >= first)


def key_window(row_start):
    key_start = max(0, row_start - (MAX_DOC + ROWS - 1) // ROWS * ROWS)
    return key_start, row_start + ROWS - key_start


def dot_t(left, right):
    return lax.dot_general(left, right, (((1,), (1,)), ((), ())), preferred_element_type=F32)


def t_dot(left, right):
    return lax.dot_general(left, right, (((0,), (0,)), ((), ())), preferred_element_type=F32)


def attend_kernel(first_ref, mixed_ref, out_ref, total_ref):
    length, group = out_ref.shape
    heads = group // HD
    scale = HD ** (-0.5)
    for row_start in range(0, length, ROWS):
        key_start, width = key_window(row_start)
        allowed = allowed_pairs(first_ref, row_start, key_start, width)
        outs = []
        totals = []
        for head in range(heads):
            at = head * HD
            query = mixed_ref[pl.ds(row_start, ROWS), pl.ds(at, HD)]
            keys = mixed_ref[pl.ds(key_start, width), pl.ds(group + at, HD)]
            values = mixed_ref[pl.ds(key_start, width), pl.ds(2 * group + at, HD)]
            scores = jnp.where(allowed, dot_t(query, keys) * scale, MASKED)
            top = jnp.max(scores, axis=1, keepdims=True)
            weights = jnp.exp(scores - top)
            total = jnp.sum(weights, axis=1, keepdims=True)
            low = (weights * (1.0 / total)).astype(BF)
            outs.append(jnp.dot(low, values, preferred_element_type=F32))
            totals.append(top + jnp.log(total))
        out_ref[pl.ds(row_start, ROWS), :] = jnp.concatenate(outs, axis=1).astype(BF)
        total_ref[pl.ds(row_start, ROWS), :] = jnp.concatenate(totals, axis=1)


def attend(first, mixed):
    length, wide = mixed.shape
    group = wide // 3
    return pl.pallas_call(
        attend_kernel,
        out_shape=(
            jax.ShapeDtypeStruct((length, group), BF),
            jax.ShapeDtypeStruct((length, group // HD), F32),
        ),
        compiler_params=pltpu.CompilerParams(vmem_limit_bytes=48 << 20),
        name="attend",
    )(first, mixed)


def attend_back_kernel(first_ref, mixed_ref, total_ref, cot_ref, out_ref, key_acc, value_acc):
    length, group = cot_ref.shape
    heads = group // HD
    scale = HD ** (-0.5)
    key_acc[...] = jnp.zeros_like(key_acc)
    value_acc[...] = jnp.zeros_like(value_acc)
    for row_start in range(0, length, ROWS):
        key_start, width = key_window(row_start)
        allowed = allowed_pairs(first_ref, row_start, key_start, width)
        query_grads = []
        key_grads = []
        value_grads = []
        for head in range(heads):
            at = head * HD
            query = mixed_ref[pl.ds(row_start, ROWS), pl.ds(at, HD)]
            keys = mixed_ref[pl.ds(key_start, width), pl.ds(group + at, HD)]
            values = mixed_ref[pl.ds(key_start, width), pl.ds(2 * group + at, HD)]
            cot = cot_ref[pl.ds(row_start, ROWS), pl.ds(at, HD)]
            total = total_ref[pl.ds(row_start, ROWS), pl.ds(head, 1)]
            scores = jnp.where(allowed, dot_t(query, keys) * scale - total, MASKED)
            probs = jnp.exp(scores)
            prob_cot = dot_t(cot, values)
            delta = jnp.sum(probs * prob_cot, axis=1, keepdims=True)
            score_cot = (probs * (prob_cot - delta)).astype(BF)
            query_grads.append(jnp.dot(score_cot, keys, preferred_element_type=F32) * scale)
            key_grads.append(t_dot(score_cot, query) * scale)
            value_grads.append(t_dot(probs.astype(BF), cot))
        out_ref[pl.ds(row_start, ROWS), pl.ds(0, group)] = jnp.concatenate(query_grads, axis=1).astype(BF)
        window = pl.ds(key_start, width)
        key_acc[window, :] += jnp.concatenate(key_grads, axis=1)
        value_acc[window, :] += jnp.concatenate(value_grads, axis=1)
    out_ref[:, pl.ds(group, group)] = key_acc[...].astype(BF)
    out_ref[:, pl.ds(2 * group, group)] = value_acc[...].astype(BF)


def attend_back(first, mixed, totals, cot):
    length, wide = mixed.shape
    group = wide // 3
    return pl.pallas_call(
        attend_back_kernel,
        out_shape=jax.ShapeDtypeStruct((length, wide), BF),
        scratch_shapes=[pltpu.VMEM((length, group), F32), pltpu.VMEM((length, group), F32)],
        compiler_params=pltpu.CompilerParams(vmem_limit_bytes=48 << 20),
        name="attend_back",
    )(first, mixed, totals, cot)


def norm_parts(values):
    center = values - jnp.mean(values, axis=-1, keepdims=True)
    inverse = lax.rsqrt(jnp.mean(center * center, axis=-1, keepdims=True) + NORM_EPS)
    return center * inverse, inverse


def norm_back(unit, inverse, gain, cot):
    scaled = cot * gain
    inner = scaled - jnp.mean(scaled, axis=-1, keepdims=True)
    inner = inner - unit * jnp.mean(scaled * unit, axis=-1, keepdims=True)
    return inner * inverse, jnp.sum(cot * unit, axis=0), jnp.sum(cot, axis=0)


def gelu_tanh(values):
    return 0.5 * values * (1.0 + jnp.tanh(0.7978845608028654 * (values + 0.044715 * values * values * values)))


def gelu_slope(values):
    square = values * values
    bent = jnp.tanh(0.7978845608028654 * (values + 0.044715 * values * square))
    inner = 0.7978845608028654 * (1.0 + 3.0 * 0.044715 * square)
    return 0.5 * (1.0 + bent) + 0.5 * values * (1.0 - bent * bent) * inner


def mul(left, right):
    return jnp.dot(left, right, preferred_element_type=F32)


def shards(tokens, norm_gains, norm_shifts, w_qkv, w_out, w_up, w_down, out_grad, doc_lengths):
    tok_rows, width = tokens.shape
    fsdp, seq = lax.axis_size("fsdp"), lax.axis_size("seq")
    ruled = fsdp == 8
    length = tok_rows * seq
    group = (H // seq) * HD
    piece = w_qkv.shape[1]
    inner = w_up.shape[2] // seq
    unit_rows = w_down.shape[1]
    place = lax.axis_index("seq")

    ends = jnp.cumsum(doc_lengths[0])
    starts = ends - doc_lengths[0]
    positions = lax.iota(jnp.int32, length)
    first = jnp.max(jnp.where(positions[:, None] >= starts[None, :], starts[None, :], 0), axis=1, keepdims=True)

    def column_parts(layer):
        qkv = w_qkv[layer].astype(BF).reshape(piece, 3, seq, group).transpose(2, 0, 1, 3)
        up = w_up[layer].astype(BF).reshape(piece, fsdp, seq, unit_rows).transpose(2, 0, 1, 3)
        return qkv.reshape(seq, piece, 3 * group), up.reshape(seq, piece, inner)

    def pad_cols(values, cols):
        return jnp.pad(values, [(0, 0)] * (values.ndim - 1) + [(0, cols - values.shape[-1])])

    def beside(columns, rows):
        rows = rows.reshape(piece, 4, group).transpose(1, 0, 2).reshape(4 * piece, group)
        return jnp.concatenate([columns, rows], axis=1)

    def apart(joined):
        rows = joined[..., 3 * group :].reshape(-1, 4, piece, group)
        return rows.transpose(0, 2, 1, 3).reshape(-1, piece, 4 * group)

    def unturn(gathered):
        rest = gathered.shape[1:]
        return gathered.reshape((4, 2) + rest).transpose((1, 0) + tuple(range(2, 2 + len(rest)))).reshape(-1, rest[-1])

    def rows_quarter(shard, size):
        whole = lax.all_gather(shard.astype(BF), BOTH, axis=0, tiled=True)
        return lax.dynamic_slice_in_dim(whole, place * size, size, 0)

    qkv_low = [None, None]
    out_low = [None, None]
    up_low = [None, None]
    down_low = [None, None]
    norms = jnp.stack([norm_gains, norm_shifts]).astype(BF).reshape(1, 1, 8 * piece)
    qkv_parts = [None, None]
    up_parts = [None, None]
    for layer in range(LAYERS):
        qkv_parts[layer], up_parts[layer] = column_parts(layer)
    sent = jnp.concatenate([qkv_parts[0], jnp.broadcast_to(pad_cols(norms, 3 * group), (seq, 8, 3 * group))], axis=1)
    early = exchange_seq(sent)
    if ruled:
        norm_rows = jnp.pad(pad_cols(early[:, piece], 4 * group), ((0, 4), (0, 0)))
        out_rows = turn(w_out.astype(BF))
        early = beside(early[:, :piece].reshape(seq * piece, 3 * group), out_rows[0])
        early = jnp.concatenate([early, norm_rows])
        attn_gather = [Gather(early), None]
        mark = attn_gather[0].advance()
    else:
        early = lax.all_gather(early, "fsdp", axis=0, tiled=False)
        qkv_low[0] = early[:, :, :piece].reshape(width, 3 * group)
        out_low[0] = rows_quarter(w_out[0], group)
        norm_low = early[:, :, piece, : 8 * piece]
        mark = []
    all_tokens = gather_seq(after(tokens, *mark))
    later = jnp.concatenate([up_parts[0], pad_cols(qkv_parts[1], inner), up_parts[1]], axis=1)
    later = exchange_seq(after(later, *mark))
    up_first = later[:, :piece].reshape(seq * piece, inner)
    qkv_next = later[:, piece : 2 * piece, : 3 * group].reshape(seq * piece, 3 * group)
    up_next = later[:, 2 * piece :].reshape(seq * piece, inner)
    if ruled:
        attn_gather[0].advance()
        mark = attn_gather[0].advance()
        low_down = w_down.astype(BF)
        mlp_gather = [
            Gather(jnp.concatenate([up_first, low_down[0]])),
            Gather(jnp.concatenate([up_next, low_down[1]])),
        ]
        attn_gather[1] = Gather(beside(qkv_next, out_rows[1]))
        mark = attn_gather[0].advance()
        mark = mlp_gather[0].advance(*mark)
        attn_gather[0].advance(*mark)
        early = attn_gather[0].result
        norm_low = early[:, 4 * piece : 4 * piece + 4, : 8 * piece]
    else:
        up_low[0] = lax.all_gather(up_first, "fsdp", axis=0, tiled=True)
        qkv_low[1] = lax.all_gather(qkv_next, "fsdp", axis=0, tiled=True)
        up_low[1] = lax.all_gather(up_next, "fsdp", axis=0, tiled=True)
        down_low[0] = lax.all_gather(w_down[0].astype(BF), "fsdp", axis=0, tiled=True)
        out_low[1] = rows_quarter(w_out[1], group)
        down_low[1] = lax.all_gather(w_down[1].astype(BF), "fsdp", axis=0, tiled=True)

    norm_low = norm_low.reshape(fsdp * seq, 2, LAYERS, 2, piece)
    norm_low = norm_low.transpose(1, 2, 3, 0, 4).reshape(2, LAYERS, 2, width).astype(F32)
    gains, shifts = norm_low[0], norm_low[1]
    def take_attn(layer):
        joined = attn_gather[layer].result[:, : 4 * piece]
        qkv_low[layer] = joined[:, :, : 3 * group].reshape(width, 3 * group)
        out_low[layer] = unturn(apart(joined))

    def take_mlp(layer):
        joined = mlp_gather[layer].result
        up_low[layer] = joined[:, : 4 * piece].reshape(width, inner)
        down_low[layer] = joined[:, 4 * piece :].reshape(inner, width)

    plan = {}
    if ruled:
        plan = {
            ("mixed", 0): [mlp_gather[0]],
            ("attended", 0): [mlp_gather[0]],
            ("scatter_a", 0): [mlp_gather[0], attn_gather[1]],
            ("gather_b", 0): [mlp_gather[0], attn_gather[1]],
            ("normed_b", 0): [attn_gather[1]],
            ("scatter_b", 0): [attn_gather[1], mlp_gather[1]],
            ("gather_a", 1): [attn_gather[1], mlp_gather[1]],
            ("mixed", 1): [mlp_gather[1]],
            ("scatter_a", 1): [mlp_gather[1]],
            ("gather_b", 1): [mlp_gather[1]],
        }

    def steps(what, layer):
        def work(gate):
            return sum([each.advance(gate) for each in plan.get((what, layer), [])], [])

        return work

    def beside_main(value, what, layer):
        moved = steps(what, layer)(value)
        return after(value, *moved)

    hidden = tokens.astype(F32)
    saved = []
    first_cot = None
    for layer in range(LAYERS):
        unit_a, inverse_a = norm_parts(hidden)
        if layer == 0:
            normed_a = (norm_parts(all_tokens.astype(F32))[0] * gains[0, 0] + shifts[0, 0]).astype(BF)
        else:
            normed_a = (unit_a * gains[layer, 0] + shifts[layer, 0]).astype(BF)
            normed_a = gather_seq(normed_a, steps("gather_a", layer))
        normed_a = beside_main(normed_a, "normed_a", layer)
        if ruled:
            take_attn(layer)
        mixed = mul(normed_a, qkv_low[layer]).astype(BF)
        if layer == LAYERS - 1:
            first_cot = gather_seq(after((BRANCH_SCALE * out_grad.astype(F32)).astype(BF), mixed))
        mixed = beside_main(mixed, "mixed", layer)
        attended, totals = attend(first, mixed)
        attended = beside_main(attended, "attended", layer)
        hidden = hidden + BRANCH_SCALE * scatter_seq(mul(attended, out_low[layer]), steps("scatter_a", layer))
        unit_b, inverse_b = norm_parts(hidden)
        normed_b = (unit_b * gains[layer, 1] + shifts[layer, 1]).astype(BF)
        normed_b = gather_seq(normed_b, steps("gather_b", layer))
        if layer == LAYERS - 1:
            normed_b = after(normed_b, first_cot)
        normed_b = beside_main(normed_b, "normed_b", layer)
        if ruled:
            take_mlp(layer)
        upper = mul(normed_b, up_low[layer])
        active = gelu_tanh(upper).astype(BF)
        hidden = hidden + BRANCH_SCALE * scatter_seq(mul(active, down_low[layer]), steps("scatter_b", layer))
        saved.append((unit_a, inverse_a, normed_a, mixed, attended, totals, unit_b, inverse_b, normed_b, upper, active))
    outputs = hidden.astype(BF)

    cot = out_grad.astype(F32)
    norm_sums = []
    column_back = {}
    row_back = {}

    def rows_blocks(grad):
        each = grad.shape[0] // 8
        return grad.reshape(2, 4, each, -1).transpose(1, 0, 2, 3).reshape(8, each, -1)

    def rows_whole(grad):
        spread = jnp.zeros((seq,) + grad.shape, BF)
        spread = lax.dynamic_update_index_in_dim(spread, grad.astype(BF), place, 0).reshape(seq * grad.shape[0], -1)
        return lax.psum_scatter(spread, BOTH, scatter_dimension=0, tiled=True).astype(F32)

    def cols_whole(grad):
        blocks = grad.astype(BF).reshape(fsdp, seq * piece, -1)
        return lax.psum_scatter(blocks, "fsdp", scatter_dimension=0, tiled=False).astype(F32)

    sums_of = {}

    def start_attn(layer, grad_qkv, grad_out):
        if not ruled:
            column_back["qkv", layer], row_back["out", layer] = cols_whole(grad_qkv), rows_whole(grad_out)
            return []
        columns = grad_qkv.astype(BF).reshape(fsdp, seq * piece, -1)
        joined = jax.vmap(beside)(columns, rows_blocks(grad_out.astype(BF)))
        sums_of["attn", layer] = Reduce(joined)
        return [joined]

    def start_mlp(layer, grad_up, grad_down):
        if not ruled:
            column_back["up", layer] = cols_whole(grad_up)
            down = grad_down.astype(BF).reshape(fsdp, unit_rows, -1)
            row_back["down", layer] = lax.psum_scatter(down, "fsdp", scatter_dimension=0, tiled=False).astype(F32)
            return []
        columns = grad_up.astype(BF).reshape(fsdp, seq * piece, -1)
        joined = jnp.concatenate([columns, grad_down.astype(BF).reshape(fsdp, unit_rows, -1)], axis=1)
        sums_of["mlp", layer] = Reduce(joined)
        return [joined]

    def step_sums(gate, *names):
        return sum([sums_of[name].advance(gate) for name in names], []) if ruled else []

    back_plan = {
        ("scatter_b", 1): [("mlp", 1)],
        ("gather_a", 1): [("mlp", 1)],
        ("scatter_a", 1): [("mlp", 1), ("attn", 1)],
        ("gather_b", 0): [("mlp", 1), ("attn", 1)],
        ("scatter_b", 0): [("mlp", 1), ("mlp", 0), ("attn", 1)],
        ("gather_a", 0): [("mlp", 0), ("attn", 1)],
        ("back", 0): [("mlp", 0), ("attn", 1)],
        ("scatter_a", 0): [("attn", 0), ("mlp", 0)],
    }
    for layer in reversed(range(LAYERS)):
        unit_a, inverse_a, normed_a, mixed, attended, totals, unit_b, inverse_b, normed_b, upper, active = saved[layer]
        if layer == LAYERS - 1:
            down_cot = first_cot
        else:
            down_cot = gather_seq(
                (BRANCH_SCALE * cot).astype(BF),
                lambda gate: step_sums(gate, *back_plan.get(("gather_b", layer), [])),
            )
        upper_cot = (gelu_slope(upper) * dot_t(down_cot, down_low[layer])).astype(BF)

        def mlp_work(gate):
            held = after(upper_cot, gate)
            moved = start_mlp(layer, t_dot(normed_b, held), t_dot(active, after(down_cot, gate)))
            return moved + step_sums(gate, *back_plan.get(("scatter_b", layer), []))

        second_cot = scatter_seq(dot_t(upper_cot, up_low[layer]), mlp_work)
        back, gain_sum_b, shift_sum_b = norm_back(unit_b, inverse_b, gains[layer, 1], second_cot)
        cot = cot + back
        attn_cot = gather_seq(
            (BRANCH_SCALE * cot).astype(BF),
            lambda gate: step_sums(gate, *back_plan.get(("gather_a", layer), [])),
        )
        attended_cot = dot_t(attn_cot, out_low[layer]).astype(BF)
        mixed_cot = attend_back(first, mixed, totals, attended_cot)
        moved = step_sums(mixed_cot, *back_plan.get(("back", layer), []))
        if moved:
            mixed_cot = after(mixed_cot, *moved)

        def attn_work(gate):
            held = after(mixed_cot, gate)
            moved = start_attn(layer, t_dot(normed_a, held), t_dot(attended, after(attn_cot, gate)))
            return moved + step_sums(gate, *back_plan.get(("scatter_a", layer), []))

        normed_cot = scatter_seq(dot_t(mixed_cot, qkv_low[layer]), attn_work)
        back, gain_sum_a, shift_sum_a = norm_back(unit_a, inverse_a, gains[layer, 0], normed_cot)
        cot = cot + back
        norm_sums.append(jnp.stack([gain_sum_a, gain_sum_b, shift_sum_a, shift_sum_b]))

    sums = jnp.concatenate(norm_sums[::-1])

    def take(layer):
        joined = sums_of["attn", layer].result
        column_back["qkv", layer], out_t = joined[:, : 3 * group], apart(joined[None])[0]
        joined = sums_of["mlp", layer].result
        column_back["up", layer] = joined[: 4 * piece]
        row_back["out", layer], row_back["down", layer] = turn(out_t.astype(BF)).astype(F32), joined[4 * piece :]

    def home(layer):
        both = jnp.concatenate([column_back["up", layer], column_back["qkv", layer]], axis=1).astype(BF)
        both = exchange_seq(both.reshape(seq, piece, -1)).astype(F32)
        qkv = both[:, :, inner:].reshape(seq, piece, 3, group).transpose(1, 2, 0, 3).reshape(piece, -1)
        up = both[:, :, :inner].reshape(seq, piece, fsdp, unit_rows).transpose(1, 2, 0, 3)
        return up.reshape(piece, -1), qkv

    if ruled:
        mark = sums_of["attn", 0].advance(sums) + sums_of["mlp", 0].advance(sums)
        take(1)
        home_1 = home(1)
        sums = after(sums, *mark)
        for bit in (1, 2):
            sums = sums + swap_seq(sums, bit)
        mark = sums_of["attn", 0].advance(sums)
        sums = after(sums, *mark)
        for bit in (1, 2):
            sums = sums + lax.ppermute(sums, "fsdp", [(f, f ^ bit) for f in range(8)])
        mark = sums_of["attn", 0].advance(sums)
        sums = after(sums, *mark)
        sums = sums + lax.ppermute(sums, "fsdp", [(f, f ^ 4) for f in range(8)])
        sums_of["attn", 0].advance(sums)
        take(0)
        home_0 = home(0)
    else:
        home_0, home_1 = home(0), home(1)
        sums = lax.psum(sums, BOTH)
    up_grads, qkv_grads = zip(home_0, home_1)
    whose = lax.axis_index("fsdp") * seq + place
    sums = lax.dynamic_slice_in_dim(sums, whose * piece, piece, 1).reshape(LAYERS, 4, piece)
    return (
        outputs,
        cot.astype(BF),
        sums[:, :2],
        sums[:, 2],
        sums[:, 3],
        jnp.stack(qkv_grads),
        jnp.stack([row_back["out", layer] for layer in range(LAYERS)]),
        jnp.stack(up_grads),
        jnp.stack([row_back["down", layer] for layer in range(LAYERS)]),
    )


def solution(mesh):
    rows = P(BOTH, None)
    thirds = P(None, None, BOTH)
    middle = P(None, BOTH, None)
    return jax.shard_map(
        shards,
        mesh=mesh,
        in_specs=(rows, thirds, thirds, middle, middle, middle, middle, rows, P("fsdp", None)),
        out_specs=(rows, rows, thirds, P(None, BOTH), P(None, BOTH), middle, middle, middle, middle),
        check_vma=False,
    )
```

```python
import functools

import jax
import jax.numpy as jnp
from jax import lax
from jax.experimental import pallas as pl
from jax.experimental.pallas import tpu as pltpu
from jax.sharding import PartitionSpec as P

H = 12
HD = 64
LAYERS = 2
MAX_DOC = 512

NORM_EPS = 1e-05
BRANCH_SCALE = 0.7071067811865476
MASKED = -1e30
BF = jnp.bfloat16
F32 = jnp.float32
BOTH = ("fsdp", "seq")

RING_NEXT = (1, 3, 0, 2)


def ring_behind(line, steps):
    at = ((line ^ (line >> 1)) - steps) & 3
    return at ^ (at >> 1)


def after(value, *others):
    return lax.optimization_barrier((value,) + others)[0] if others else value


def swap_seq(values, bit):
    return lax.ppermute(values, "seq", [(s, s ^ bit) for s in range(4)])


def by_bit(bit, own, other):
    zero = bit == 0
    return jnp.where(zero, own, other), jnp.where(zero, other, own)


def gather_seq(rows, work=None):
    far = swap_seq(rows, 2)
    near = swap_seq(rows, 1)
    if work is not None:
        far = after(far, *work(rows))
    return [rows, far, near, swap_seq(far, 1)]


def scatter_seq(sent, kept, work=None):
    half = kept + swap_seq(sent, 1).astype(F32)
    sent = half[1].astype(BF)
    got = swap_seq(sent, 2)
    if work is not None:
        got = after(got, *work(sent))
    return half[0] + got.astype(F32)


def exchange_seq(parts):
    place = lax.axis_index("seq")
    y_bit, c_bit = place // 2, place % 2
    grid = parts.reshape((2, 2) + parts.shape[1:])
    kept, sent = by_bit(c_bit, grid[:, 0], grid[:, 1])
    half = jnp.stack(by_bit(c_bit, kept, swap_seq(sent, 1)), axis=1)
    kept, sent = by_bit(y_bit, half[0], half[1])
    return jnp.stack(by_bit(y_bit, kept, swap_seq(sent, 2))).reshape(parts.shape)


def over_line(block, steps=1):
    moves = []
    for f in range(8):
        line = f // 2
        for _ in range(steps):
            line = RING_NEXT[line]
        moves.append((f, 2 * line + f % 2))
    return lax.ppermute(block, "fsdp", moves)


def over_side(block):
    return lax.ppermute(block, "fsdp", [(f, f ^ 1) for f in range(8)])


def owner(steps, other=0):
    place = lax.axis_index("fsdp")
    return 2 * ring_behind(place // 2, steps) + (place % 2 ^ other)


def owners():
    count = lax.axis_size("fsdp")
    if count != 8:
        return jnp.arange(8, dtype=jnp.int32)
    return jnp.stack([owner(steps, other) for other in (0, 1) for steps in range(4)]).astype(jnp.int32)


class Gather:
    def __init__(self, block):
        self.blocks = [block]
        self.sides = []

    def advance(self, *gates):
        block = after(self.blocks[-1], *gates)
        moved = [over_side(block)]
        self.sides.append(moved[0])
        if len(self.sides) < 4:
            moved.append(over_line(block))
            self.blocks.append(moved[1])
        return moved

    def result(self):
        return self.blocks + self.sides


class Reduce:
    def __init__(self, blocks):
        self.blocks = blocks
        self.step = 0
        self.got = 0.0

    def advance(self, *gates):
        self.step += 1
        moved = [over_side(after(self.blocks[4 + self.step % 4], *gates))]
        if self.step > 1:
            moved.append(over_line(after(self.total.astype(BF), *gates)))
            self.got = moved[1].astype(F32)
        self.total = self.got + moved[0].astype(F32) + self.blocks[self.step % 4].astype(F32)
        return moved


def turn(rows):
    moves = []
    for f in range(8):
        for s in range(4):
            moves.append((f * 4 + s, (2 * s + f % 2) * 4 + f // 2))
    return lax.ppermute(rows, BOTH, moves)


ROWS = 256


def allowed_pairs(first_ref, row_start, key_start, width):
    key_pos = key_start + lax.broadcasted_iota(jnp.int32, (ROWS, width), 1)
    query_pos = row_start + lax.broadcasted_iota(jnp.int32, (ROWS, width), 0)
    first = first_ref[pl.ds(row_start, ROWS), :]
    return (key_pos <= query_pos) & (key_pos >= first)


def key_window(row_start):
    key_start = max(0, row_start - (MAX_DOC + ROWS - 1) // ROWS * ROWS)
    return key_start, row_start + ROWS - key_start


def dot_t(left, right):
    return lax.dot_general(left, right, (((1,), (1,)), ((), ())), preferred_element_type=F32)


def t_dot(left, right):
    return lax.dot_general(left, right, (((0,), (0,)), ((), ())), preferred_element_type=F32)


def parts_of(refs):
    return [ref.at[pl.ds(at, ROWS)] for ref in refs for at in range(0, ref.shape[0], ROWS)]


def row_starts(place_ref):
    return [pl.multiple_of((place_ref[0] ^ bits) * ROWS, ROWS) for bits in (0, 2, 1, 3)]


def put_part(sent_ref, kept_ref, part, values):
    if part < 2:
        kept_ref[part] = values
    else:
        sent_ref[part - 2] = values.astype(BF)


def place_blocks(info_ref, blocks, places):
    for slot, block in enumerate(blocks):
        at = info_ref[1 + slot]
        for target, first_row, rows, cols, turned in places:
            where = (at % 2 * 4 + at // 2) if turned else at
            values = block[pl.ds(first_row, rows), pl.ds(0, cols)].astype(target.dtype)
            target[pl.ds(pl.multiple_of(where * rows, 8 if turned else 32), rows), :] = values


def attend_places(blocks, qkv_weight, out_weight):
    top, each = qkv_weight.shape[0] // 8, out_weight.shape[0] // 8
    width = out_weight.shape[1]
    return [(qkv_weight, 0, top, qkv_weight.shape[1], False), (out_weight, top, each, width, True)]


def feed_places(up_weight, down_weight):
    each, width = up_weight.shape[0] // 8, up_weight.shape[1]
    return [(up_weight, 0, each, width, False), (down_weight, each, each, width, False)]


def attend_kernel(place_ref, first_ref, *refs):
    blocks, parts = refs[:8], parts_of(refs[8:-7])
    mixed_ref, attended_ref, total_ref, sent_ref, kept_ref, qkv_weight, out_weight = refs[-7:]
    length, group = attended_ref.shape
    heads = group // HD
    scale = jnp.asarray(HD ** (-0.5), BF)
    starts = row_starts(place_ref)
    place_blocks(place_ref, blocks, attend_places(blocks, qkv_weight, out_weight))
    weight = qkv_weight[...]
    for part, start in zip(parts, starts):
        mixed_ref[pl.ds(start, ROWS), :] = jnp.dot(part[...], weight, preferred_element_type=F32).astype(BF)
    for row_start in range(0, length, ROWS):
        key_start, width = key_window(row_start)
        allowed = allowed_pairs(first_ref, row_start, key_start, width)
        outs = []
        totals = []
        for head in range(heads):
            at = head * HD
            query = mixed_ref[pl.ds(row_start, ROWS), pl.ds(at, HD)] * scale
            keys = mixed_ref[pl.ds(key_start, width), pl.ds(group + at, HD)]
            values = mixed_ref[pl.ds(key_start, width), pl.ds(2 * group + at, HD)]
            scores = jnp.where(allowed, dot_t(query, keys), MASKED)
            top = jnp.max(scores, axis=1, keepdims=True)
            weights = jnp.exp(scores - top)
            total = jnp.sum(weights, axis=1, keepdims=True)
            low = (weights * (1.0 / total)).astype(BF)
            outs.append(jnp.dot(low, values, preferred_element_type=F32))
            totals.append(top + jnp.log(total))
        attended_ref[pl.ds(row_start, ROWS), :] = jnp.concatenate(outs, axis=1).astype(BF)
        total_ref[pl.ds(row_start, ROWS), :] = jnp.concatenate(totals, axis=1)
    weight = out_weight[...].astype(BF)
    for part, start in enumerate(starts):
        values = jnp.dot(attended_ref[pl.ds(start, ROWS), :], weight, preferred_element_type=F32)
        put_part(sent_ref, kept_ref, part, values)


TAKES = {"attend": 10, "attend_back": 14, "attend_sum": 5, "feed": 5, "feed_back": 8, "feed_sum": 6}


def call(kernel, name, outs, scratch, *args):
    in_specs = [pl.BlockSpec(memory_space=pltpu.SMEM)] + [pl.BlockSpec(memory_space=pltpu.VMEM)] * (len(args) - 1)
    return pl.pallas_call(
        kernel,
        in_specs=in_specs,
        out_shape=tuple(jax.ShapeDtypeStruct(shape, dtype) for shape, dtype in outs),
        scratch_shapes=[pltpu.VMEM(shape, dtype) for shape, dtype in scratch],
        cost_estimate=pl.CostEstimate(flops=TAKES[name] * 10**9, bytes_accessed=TAKES[name] * 3 * 10**6, transcendentals=0),
        compiler_params=pltpu.CompilerParams(vmem_limit_bytes=56 << 20),
        name=name,
    )(*args)


def two_parts(width):
    return [((2, ROWS, width), BF), ((2, ROWS, width), F32)]


def attend(place, first, blocks, parts, group):
    length, width = first.shape[0], blocks[0].shape[1]
    outs = [((length, 3 * group), BF), ((length, group), BF), ((length, group // HD), F32)] + two_parts(width)
    scratch = [((width, 3 * group), BF), ((group, width), F32)]
    return call(attend_kernel, "attend", outs, scratch, place, first, *blocks, *parts)


def attend_back_kernel(place_ref, first_ref, mixed_ref, total_ref, *refs):
    blocks, parts = refs[:8], parts_of(refs[8:-8])
    out_ref, sent_ref, kept_ref, qkv_weight, out_weight, cot_ref, key_acc, value_acc = refs[-8:]
    length, group = key_acc.shape
    heads = group // HD
    scale = jnp.asarray(HD ** (-0.5), BF)
    starts = row_starts(place_ref)
    place_blocks(place_ref, blocks, attend_places(blocks, qkv_weight, out_weight))
    weight = out_weight[...].astype(BF)
    for part, start in zip(parts, starts):
        cot_ref[pl.ds(start, ROWS), :] = dot_t(part[...], weight)
    key_acc[...] = jnp.zeros_like(key_acc)
    value_acc[...] = jnp.zeros_like(value_acc)
    for row_start in range(0, length, ROWS):
        key_start, width = key_window(row_start)
        allowed = allowed_pairs(first_ref, row_start, key_start, width)
        query_grads = []
        key_grads = []
        value_grads = []
        for head in range(heads):
            at = head * HD
            query = mixed_ref[pl.ds(row_start, ROWS), pl.ds(at, HD)] * scale
            keys = mixed_ref[pl.ds(key_start, width), pl.ds(group + at, HD)]
            values = mixed_ref[pl.ds(key_start, width), pl.ds(2 * group + at, HD)]
            cot = cot_ref[pl.ds(row_start, ROWS), pl.ds(at, HD)].astype(BF)
            total = total_ref[pl.ds(row_start, ROWS), pl.ds(head, 1)]
            scores = jnp.where(allowed, dot_t(query, keys) - total, MASKED)
            probs = jnp.exp(scores)
            prob_cot = dot_t(cot, values)
            delta = jnp.sum(probs * prob_cot, axis=1, keepdims=True)
            score_cot = (probs * (prob_cot - delta)).astype(BF)
            query_grads.append(jnp.dot(score_cot, keys, preferred_element_type=F32) * scale)
            key_grads.append(t_dot(score_cot, query))
            value_grads.append(t_dot(probs.astype(BF), cot))
        out_ref[pl.ds(row_start, ROWS), pl.ds(0, group)] = jnp.concatenate(query_grads, axis=1).astype(BF)
        window = pl.ds(key_start, width)
        key_acc[window, :] += jnp.concatenate(key_grads, axis=1)
        value_acc[window, :] += jnp.concatenate(value_grads, axis=1)
    out_ref[:, pl.ds(group, group)] = key_acc[...].astype(BF)
    out_ref[:, pl.ds(2 * group, group)] = value_acc[...].astype(BF)
    weight = qkv_weight[...]
    for part, start in enumerate(starts):
        put_part(sent_ref, kept_ref, part, dot_t(out_ref[pl.ds(start, ROWS), :], weight))


def attend_back(place, first, blocks, mixed, totals, parts):
    length, wide = mixed.shape
    group, width = wide // 3, blocks[0].shape[1]
    outs = [((length, wide), BF)] + two_parts(width)
    scratch = [((width, wide), BF), ((group, width), F32)] + [((length, group), F32)] * 3
    return call(attend_back_kernel, "attend_back", outs, scratch, place, first, mixed, totals, *blocks, *parts)


def joint(parts):
    return jnp.concatenate([part[...] for part in parts], axis=0)


def attend_sum_kernel(count, place_ref, mixed_cot_ref, attended_ref, *refs):
    normed, cots = parts_of(refs[:count]), parts_of(refs[count:-10])
    outs, qkv_grad, out_grad = refs[-10:-2], refs[-2], refs[-1]
    width, wide = qkv_grad.shape
    top, each = width // 8, out_grad.shape[0] // 8
    starts = row_starts(place_ref)
    mixed_cot = jnp.concatenate([mixed_cot_ref[pl.ds(start, ROWS), :] for start in starts], axis=0)
    qkv_grad[...] = t_dot(joint(normed), mixed_cot).astype(BF)
    attended = jnp.concatenate([attended_ref[pl.ds(start, ROWS), :] for start in starts], axis=0)
    out_grad[...] = t_dot(attended, joint(cots))
    for slot, out in enumerate(outs):
        at = place_ref[1 + slot]
        out[pl.ds(0, top), :] = jnp.zeros((top, width), BF)
        out[pl.ds(0, top), pl.ds(0, wide)] = qkv_grad[pl.ds(pl.multiple_of(at * top, 32), top), :]
        turned = pl.multiple_of((at % 2 * 4 + at // 2) * each, 8)
        out[pl.ds(top, each), :] = out_grad[pl.ds(turned, each), :].astype(BF)


def attend_sum(place, mixed_cot, attended, normed, cots):
    width, group = cots[0].shape[1], attended.shape[1]
    kernel = functools.partial(attend_sum_kernel, len(normed))
    outs = [((width // 8 + group // 8, width), BF)] * 8
    scratch = [((width, 3 * group), BF), ((group, width), F32)]
    return call(kernel, "attend_sum", outs, scratch, place, mixed_cot, attended, *normed, *cots)


def gelu_tanh(values):
    return 0.5 * values * (1.0 + jnp.tanh(0.7978845608028654 * (values + 0.044715 * values * values * values)))


def feed_kernel(place_ref, *refs):
    blocks, parts = refs[:8], parts_of(refs[8:-4])
    sent_ref, kept_ref, up, down = refs[-4:]
    place_blocks(place_ref, blocks, feed_places(up, down))
    for at, part in enumerate(parts):
        active = gelu_tanh(jnp.dot(part[...], up[...], preferred_element_type=F32)).astype(BF)
        put_part(sent_ref, kept_ref, at, jnp.dot(active, down[...], preferred_element_type=F32))


def feed_scratch(blocks):
    rows, width = blocks[0].shape
    return [((4 * rows, width), BF)] * 2


def feed(place, blocks, parts):
    return call(feed_kernel, "feed", two_parts(blocks[0].shape[1]), feed_scratch(blocks), place, *blocks, *parts)


def feed_back_kernel(place_ref, *refs):
    blocks, refs, (active_ref, cot_ref, sent_ref, kept_ref, up, down) = refs[:8], refs[8:-6], refs[-6:]
    normed, cots = parts_of(refs[: len(refs) // 2]), parts_of(refs[len(refs) // 2 :])
    place_blocks(place_ref, blocks, feed_places(up, down))
    for at, (part, cot) in enumerate(zip(normed, cots)):
        upper = jnp.dot(part[...], up[...], preferred_element_type=F32)
        square = upper * upper
        bent = jnp.tanh(0.7978845608028654 * (upper + 0.044715 * upper * square))
        inner = 0.7978845608028654 * (1.0 + 3.0 * 0.044715 * square)
        half_up = 0.5 * upper
        rows = pl.ds(at * ROWS, ROWS)
        active_ref[rows, :] = (half_up * (1.0 + bent)).astype(BF)
        slope = 0.5 * (1.0 + bent) + half_up * (1.0 - bent * bent) * inner
        upper_cot = (slope * dot_t(cot[...], down[...])).astype(BF)
        cot_ref[rows, :] = upper_cot
        put_part(sent_ref, kept_ref, at, dot_t(upper_cot, up[...]))


def feed_back(place, blocks, normed, cots):
    rows, width = blocks[0].shape
    outs = [((4 * ROWS, 4 * rows), BF)] * 2 + two_parts(width)
    return call(feed_back_kernel, "feed_back", outs, feed_scratch(blocks), place, *blocks, *normed, *cots)


def feed_sum_kernel(place_ref, active_ref, upper_cot_ref, *refs):
    outs, up_grad, down_grad = refs[-10:-2], refs[-2], refs[-1]
    refs = refs[:-10]
    normed, cots = parts_of(refs[: len(refs) // 2]), parts_of(refs[len(refs) // 2 :])
    each = up_grad.shape[0] // 8
    up_grad[...] = t_dot(joint(normed), upper_cot_ref[...]).astype(BF)
    down_grad[...] = t_dot(active_ref[...], joint(cots)).astype(BF)
    for slot, out in enumerate(outs):
        rows = pl.ds(pl.multiple_of(place_ref[1 + slot] * each, 32), each)
        out[pl.ds(0, each), :] = up_grad[rows, :]
        out[pl.ds(each, each), :] = down_grad[rows, :]


def feed_sum(place, active, upper_cot, normed, cots):
    width, inner = cots[0].shape[1], active.shape[1]
    outs = [((inner // 4, width), BF)] * 8
    scratch = [((width, inner), BF), ((inner, width), BF)]
    return call(feed_sum_kernel, "feed_sum", outs, scratch, place, active, upper_cot, *normed, *cots)


def store_kernel(fsdp, *refs):
    qkv_out, out_out, up_out, down_out = refs[6:]
    for layer in range(LAYERS):
        columns_ref, rows_ref, fed_ref = refs[3 * layer : 3 * layer + 3]
        out_out[layer] = rows_ref[...].astype(F32)
        down_out[layer] = fed_ref[pl.ds(fed_ref.shape[0] - down_out.shape[1], down_out.shape[1]), :]
        seq = columns_ref.shape[0]
        inner, group = up_out.shape[2] // seq, qkv_out.shape[2] // (3 * seq)
        for quarter in range(seq):
            values = columns_ref[quarter].astype(F32)
            each = inner // fsdp
            for part in range(fsdp):
                at = (part * seq + quarter) * each
                up_out[layer, :, pl.ds(at, each)] = values[:, part * each : part * each + each]
            for part in range(3):
                at = (part * seq + quarter) * group
                start = inner + part * group
                qkv_out[layer, :, pl.ds(at, group)] = values[:, start : start + group]


def store(sent_0, sent_1, group, seq, fsdp):
    piece, width = sent_0[1].shape
    inner = sent_0[0].shape[2] - 3 * group
    shapes = [(piece, 3 * group * seq), (piece, width), (piece, inner * seq), (inner * seq // (fsdp * seq), width)]
    outs = [((LAYERS,) + shape, F32) for shape in shapes]
    args = sent_0 + sent_1
    return pl.pallas_call(
        functools.partial(store_kernel, fsdp),
        out_shape=tuple(jax.ShapeDtypeStruct(shape, dtype) for shape, dtype in outs),
        compiler_params=pltpu.CompilerParams(vmem_limit_bytes=56 << 20),
        name="store",
    )(*args)


def norm_parts(values):
    center = values - jnp.mean(values, axis=-1, keepdims=True)
    inverse = lax.rsqrt(jnp.mean(center * center, axis=-1, keepdims=True) + NORM_EPS)
    return center * inverse, inverse


def norm_back(unit, inverse, gain, cot):
    scaled = cot * gain
    inner = scaled - jnp.mean(scaled, axis=-1, keepdims=True)
    inner = inner - unit * jnp.mean(scaled * unit, axis=-1, keepdims=True)
    return inner * inverse, jnp.sum(cot * unit, axis=0), jnp.sum(cot, axis=0)


NORM_AT = 640


def norm_kernel(place_ref, *refs):
    blocks, out_ref, both = refs[:8], refs[8], refs[9]
    each = both.shape[0] // 8
    for slot, block in enumerate(blocks):
        both[pl.ds(pl.multiple_of(place_ref[1 + slot] * each, 32), each), :] = block[...].astype(F32)
    out_ref[...] = both[...].T[:8]


def norms_of(place, blocks):
    width = blocks[0].shape[1]
    part = pl.BlockSpec((width // 8, 128), lambda step: (0, NORM_AT // 128))
    return pl.pallas_call(
        norm_kernel,
        grid=(1,),
        in_specs=[pl.BlockSpec(memory_space=pltpu.SMEM)] + [part] * 8,
        out_shape=jax.ShapeDtypeStruct((8, width), F32),
        scratch_shapes=[pltpu.VMEM((width, 128), F32)],
        name="norms_of",
    )(place, *blocks)


def shards(tokens, norm_gains, norm_shifts, w_qkv, w_out, w_up, w_down, out_grad, doc_lengths):
    tok_rows, width = tokens.shape
    fsdp, seq = lax.axis_size("fsdp"), lax.axis_size("seq")
    ruled = fsdp == 8
    length = tok_rows * seq
    group = (H // seq) * HD
    piece = w_qkv.shape[1]
    inner = w_up.shape[2] // seq
    unit_rows = w_down.shape[1]
    place = lax.axis_index("seq")

    ends = jnp.cumsum(doc_lengths[0])
    starts = ends - doc_lengths[0]
    positions = lax.iota(jnp.int32, length)
    first = jnp.max(jnp.where(positions[:, None] >= starts[None, :], starts[None, :], 0), axis=1, keepdims=True)

    def column_parts(layer):
        qkv = w_qkv[layer].astype(BF).reshape(piece, 3, seq, group).transpose(2, 0, 1, 3)
        up = w_up[layer].astype(BF).reshape(piece, fsdp, seq, unit_rows).transpose(2, 0, 1, 3)
        return qkv.reshape(seq, piece, 3 * group), up.reshape(seq, piece, inner)

    def pad_cols(values, cols):
        return jnp.pad(values, [(0, 0)] * (values.ndim - 1) + [(0, cols - values.shape[-1])])

    place_ref = jnp.concatenate([place.reshape(1).astype(jnp.int32), owners()])
    norms = jnp.stack([norm_gains, norm_shifts]).astype(BF).reshape(8, piece).T
    norms = jnp.pad(norms, ((0, 0), (NORM_AT - 3 * group, width - NORM_AT - 8)))
    qkv_parts = [None, None]
    up_parts = [None, None]
    for layer in range(LAYERS):
        qkv_parts[layer], up_parts[layer] = column_parts(layer)
    early = jnp.concatenate([qkv_parts[0], jnp.broadcast_to(norms[None], (seq,) + norms.shape)], axis=2)
    early = exchange_seq(early).reshape(seq * piece, width)
    attn_low = [None, None]
    feed_low = [None, None]

    def wide_blocks(values):
        return pad_cols(values.reshape(8, -1, values.shape[-1]), width)

    def out_blocks(rows):
        return rows.reshape(2, 4, -1, width).transpose(1, 0, 2, 3).reshape(8, -1, width)

    def out_rows_of(blocks):
        return blocks.reshape(4, 2, -1, width).transpose(1, 0, 2, 3).reshape(-1, width)

    if ruled:
        out_rows = turn(w_out.astype(BF))
        early = jnp.concatenate([early, out_rows[0]])
        mark = [early]
        first_gather = Gather(early)
        first_moved = first_gather.advance()
    else:
        mark = []
        first_steps = []
    all_tokens = gather_seq(after(tokens, *mark))
    later = jnp.concatenate([up_parts[0], pad_cols(qkv_parts[1], inner), up_parts[1]], axis=1)
    later = exchange_seq(after(later, *mark))
    up_first = later[:, :piece].reshape(seq * piece, inner)
    qkv_next = later[:, piece : 2 * piece].reshape(seq * piece, inner)
    up_next = later[:, 2 * piece :].reshape(seq * piece, inner)
    if ruled:
        first_moved = first_gather.advance(*first_moved)
        low_down = w_down.astype(BF)
        feed_gather = [
            Gather(jnp.concatenate([up_first, low_down[0]])),
            Gather(jnp.concatenate([up_next, low_down[1]])),
        ]
        attn_gather = Gather(jnp.concatenate([qkv_next, out_rows[1]]))
        first_gather.advance(feed_gather[0].blocks[0], *first_moved)
        moved = feed_gather[0].advance(*first_moved)
        first_gather.advance(first_gather.sides[2])
        first_steps = feed_gather[0].advance(first_gather.blocks[3], *moved)
        attn_low[0] = first_gather.result()
    else:
        early = lax.all_gather(early, "fsdp", axis=0, tiled=True)

        def gathered(columns):
            return lax.all_gather(columns, "fsdp", axis=0, tiled=True)

        def attn_joined(columns, rows):
            rows = lax.all_gather(rows.astype(BF), BOTH, axis=0, tiled=True)
            rows = lax.dynamic_slice_in_dim(rows, place * group, group, 0)
            return jnp.concatenate([columns.reshape(8, -1, width), out_blocks(rows)], axis=1)

        attn_low = [list(attn_joined(early, w_out[0])), list(attn_joined(gathered(qkv_next), w_out[1]))]
        for layer, columns in enumerate((up_first, up_next)):
            blocks = gathered(columns), gathered(w_down[layer].astype(BF))
            feed_low[layer] = list(jnp.concatenate([wide_blocks(part) for part in blocks], axis=1))

    norm_low = norms_of(place_ref, attn_low[0]).reshape(2, LAYERS, 2, width)
    gains, shifts = norm_low[0], norm_low[1]

    plan = {}
    if ruled:
        plan = {
            ("scatter_a", 0): [feed_gather[0], attn_gather],
            ("gather_b", 0): [feed_gather[0], attn_gather],
            ("scatter_b", 0): [attn_gather, feed_gather[1]],
            ("gather_a", 1): [attn_gather, feed_gather[1]],
            ("scatter_a", 1): [feed_gather[1]],
            ("gather_b", 1): [feed_gather[1]],
        }

    def steps(what, layer):
        def work(gate):
            return sum([each.advance(gate) for each in plan.get((what, layer), [])], [])

        return work

    def beside_main(value, what, layer):
        moved = steps(what, layer)(value)
        return after(value, *moved)

    first_cot = gather_seq(after((BRANCH_SCALE * out_grad.astype(F32)).astype(BF), all_tokens[1]))
    first_steps = first_steps + first_cot[1:]

    hidden = tokens.astype(F32)
    saved = []
    for layer in range(LAYERS):
        unit_a, inverse_a = norm_parts(hidden)
        if layer == 0:
            normed_a = (norm_parts(jnp.concatenate(all_tokens).astype(F32))[0] * gains[0, 0] + shifts[0, 0]).astype(BF)
            normed_a = [after(normed_a, *first_steps)]
        else:
            normed_a = (unit_a * gains[layer, 0] + shifts[layer, 0]).astype(BF)
            normed_a = gather_seq(normed_a, steps("gather_a", layer))
        normed_a[-1] = beside_main(normed_a[-1], "normed_a", layer)
        if ruled and layer > 0:
            attn_low[layer] = attn_gather.result()
        mixed, attended, totals, sent, kept = attend(place_ref, first, attn_low[layer], normed_a, group)
        sent = beside_main(sent, "attended", layer)
        hidden = hidden + BRANCH_SCALE * scatter_seq(sent, kept, steps("scatter_a", layer))
        unit_b, inverse_b = norm_parts(hidden)
        normed_b = (unit_b * gains[layer, 1] + shifts[layer, 1]).astype(BF)
        normed_b = gather_seq(normed_b, steps("gather_b", layer))
        normed_b[-1] = beside_main(normed_b[-1], "normed_b", layer)
        if ruled:
            feed_low[layer] = feed_gather[layer].result()
        if layer < LAYERS - 1:
            sent, kept = feed(place_ref, feed_low[layer], normed_b)
            hidden = hidden + BRANCH_SCALE * scatter_seq(sent, kept, steps("scatter_b", layer))
        saved.append((unit_a, inverse_a, normed_a, mixed, attended, totals, unit_b, inverse_b, normed_b))
    last_feed = []

    cot = out_grad.astype(F32)
    norm_sums = []
    sums_of = {}
    grads_of = {}

    def start_sum(name, blocks):
        if ruled:
            sums_of[name] = Reduce(blocks)
        else:
            grads_of[name] = jnp.stack(blocks)
        return [blocks[0]]

    def step_sums(gate, *names):
        return sum([sums_of[name].advance(gate) for name in names], []) if ruled else []

    back_plan = {
        ("gather_a", 1): [("feed", 1)],
        ("scatter_a", 1): [("feed", 1)],
        ("gather_b", 0): [("feed", 1), ("attn", 1)],
        ("scatter_b", 0): [("feed", 1), ("attn", 1)],
        ("gather_a", 0): [("feed", 0), ("attn", 1)],
        ("scatter_a", 0): [("feed", 0), ("attn", 1)],
        ("after_sum", 0): [("attn", 0)],
    }
    for layer in reversed(range(LAYERS)):
        unit_a, inverse_a, normed_a, mixed, attended, totals, unit_b, inverse_b, normed_b = saved[layer]

        def sum_steps(what):
            return lambda gate: step_sums(gate, *back_plan.get((what, layer), []))

        if layer == LAYERS - 1:
            down_cot = first_cot
        else:
            down_cot = gather_seq((BRANCH_SCALE * cot).astype(BF), sum_steps("gather_b"))
        active, upper_cot, sent, kept = feed_back(place_ref, feed_low[layer], normed_b, down_cot)

        def feed_work(gate):
            moved = start_sum(("feed", layer), feed_sum(place_ref, after(active, gate), upper_cot, normed_b, down_cot))
            return moved + sum_steps("scatter_b")(gate)

        second_cot = scatter_seq(sent, kept, feed_work)
        back, gain_sum_b, shift_sum_b = norm_back(unit_b, inverse_b, gains[layer, 1], second_cot)
        cot = cot + back

        def norm_work(gate):
            if layer == LAYERS - 1:
                parts = [after(normed_b[0], gate)] + normed_b[1:]
                last_feed.extend(feed(place_ref, feed_low[layer], parts))
            return sum_steps("gather_a")(gate) + last_feed[:1]

        attn_cot = gather_seq((BRANCH_SCALE * cot).astype(BF), norm_work)
        mixed_cot, sent, kept = attend_back(place_ref, first, attn_low[layer], mixed, totals, attn_cot)
        sent = after(sent, *sum_steps("back")(mixed_cot))

        def attn_work(gate):
            joined = attend_sum(place_ref, after(mixed_cot, gate), attended, normed_a, attn_cot)
            moved = sum_steps("scatter_a")(gate) + start_sum(("attn", layer), joined)
            return moved + sum_steps("after_sum")(gate)

        normed_cot = scatter_seq(sent, kept, attn_work)
        back, gain_sum_a, shift_sum_a = norm_back(unit_a, inverse_a, gains[layer, 0], normed_cot)
        cot = cot + back
        norm_sums.append(jnp.stack([gain_sum_a, gain_sum_b, shift_sum_a, shift_sum_b]))

    sent, kept = last_feed
    outputs = (hidden + BRANCH_SCALE * scatter_seq(after(sent, cot), kept)).astype(BF)
    sums = jnp.concatenate(norm_sums[::-1])
    column_back = {}
    row_back = {}

    def send_home(layer, *gates):
        attn, fed = sums_of["attn", layer].total, sums_of["feed", layer].total
        columns = jnp.concatenate([fed[: seq * piece], attn[: seq * piece, : 3 * group]], axis=1).astype(BF)
        rows = after(attn[seq * piece :].astype(BF), *gates)
        columns = exchange_seq(after(columns, *gates).reshape(seq, piece, -1))
        return columns, turn(rows), fed

    def take(layer):
        def summed(blocks):
            return lax.psum_scatter(blocks, "fsdp", scatter_dimension=0, tiled=True).astype(F32)

        joined = grads_of["attn", layer]
        column_back["qkv", layer] = summed(joined[:, : width // 8, : 3 * group].reshape(width, 3 * group))
        rows = out_rows_of(joined[:, width // 8 :])
        spread = jnp.zeros((seq,) + rows.shape, BF)
        spread = lax.dynamic_update_index_in_dim(spread, rows, place, 0).reshape(-1, width)
        row_back["out", layer] = lax.psum_scatter(spread, BOTH, scatter_dimension=0, tiled=True).astype(F32)
        joined = grads_of["feed", layer]
        column_back["up", layer] = summed(joined[:, : width // 8].reshape(width, inner))
        row_back["down", layer] = summed(joined[:, width // 8 :].reshape(inner, width))

    def home(layer):
        both = jnp.concatenate([column_back["up", layer], column_back["qkv", layer]], axis=1).astype(BF)
        both = exchange_seq(both.reshape(seq, piece, -1)).astype(F32)
        qkv = both[:, :, inner:].reshape(seq, piece, 3, group).transpose(1, 2, 0, 3).reshape(piece, -1)
        up = both[:, :, :inner].reshape(seq, piece, fsdp, unit_rows).transpose(1, 2, 0, 3)
        return up.reshape(piece, -1), qkv

    if ruled:
        mark = sums_of["attn", 0].advance() + sums_of["feed", 0].advance() + [outputs]
        for bit in (1, 2):
            sums = sums + swap_seq(sums, bit)
        sums = after(sums, *mark)
        mark = step_sums(sums, ("attn", 0), ("feed", 0))
        sent_1 = send_home(1, sums)
        for bit in (1, 2):
            sums = sums + lax.ppermute(sums, "fsdp", [(f, f ^ bit) for f in range(8)])
        sums = after(sums, *mark)
        step_sums(sums, ("attn", 0))
        sums = sums + lax.ppermute(sums, "fsdp", [(f, f ^ 4) for f in range(8)])
        weight_grads = store(send_home(0), sent_1, group, seq, fsdp)
    else:
        take(0)
        take(1)
        home_0, home_1 = home(0), home(1)
        sums = lax.psum(sums, BOTH)
        up_grads, qkv_grads = zip(home_0, home_1)
        out_grads = [row_back["out", layer] for layer in range(LAYERS)]
        down_grads = [row_back["down", layer] for layer in range(LAYERS)]
        weight_grads = [jnp.stack(grads) for grads in (qkv_grads, out_grads, up_grads, down_grads)]
    whose = lax.axis_index("fsdp") * seq + place
    sums = lax.dynamic_slice_in_dim(sums, whose * piece, piece, 1).reshape(LAYERS, 4, piece)
    return (
        outputs,
        cot.astype(BF),
        sums[:, :2],
        sums[:, 2],
        sums[:, 3],
        *weight_grads,
    )


def solution(mesh):
    rows = P(BOTH, None)
    thirds = P(None, None, BOTH)
    middle = P(None, BOTH, None)
    return jax.shard_map(
        shards,
        mesh=mesh,
        in_specs=(rows, thirds, thirds, middle, middle, middle, middle, rows, P("fsdp", None)),
        out_specs=(rows, rows, thirds, P(None, BOTH), P(None, BOTH), middle, middle, middle, middle),
        check_vma=False,
    )
```

```python
import functools

import jax
import jax.numpy as jnp
from jax import lax
from jax.experimental import pallas as pl
from jax.experimental.pallas import tpu as pltpu
from jax.sharding import PartitionSpec as P

H = 12
HD = 64
LAYERS = 2
MAX_DOC = 512

NORM_EPS = 1e-05
BRANCH_SCALE = 0.7071067811865476
MASKED = -1e30
BF = jnp.bfloat16
F32 = jnp.float32
BOTH = ("fsdp", "seq")

RING_NEXT = (1, 3, 0, 2)


def ring_behind(line, steps):
    at = ((line ^ (line >> 1)) - steps) & 3
    return at ^ (at >> 1)


def after(value, *others):
    return lax.optimization_barrier((value,) + others)[0] if others else value


def swap_seq(values, bit):
    return lax.ppermute(values, "seq", [(s, s ^ bit) for s in range(4)])


def by_bit(bit, own, other):
    zero = bit == 0
    return jnp.where(zero, own, other), jnp.where(zero, other, own)


def gather_seq(rows, work=None):
    far = swap_seq(rows, 2)
    near = swap_seq(rows, 1)
    if work is not None:
        far = after(far, *work(rows))
    return [rows, far, near, swap_seq(far, 1)]


def scatter_seq(sent, kept, work=None):
    half = kept.astype(F32) + swap_seq(sent, 1).astype(F32)
    sent = half[1].astype(BF)
    got = swap_seq(sent, 2)
    if work is not None:
        got = after(got, *work(sent))
    return half[0] + got.astype(F32)


def exchange_seq(parts):
    place = lax.axis_index("seq")
    own = [lax.dynamic_index_in_dim(parts, place ^ bits, 0, keepdims=False) for bits in range(4)]
    got = own[:1] + [swap_seq(own[bits], bits) for bits in (1, 2, 3)]
    core = place % 2 == 0
    pairs = [(jnp.where(core, got[at], got[at + 1]), jnp.where(core, got[at + 1], got[at])) for at in (0, 2)]
    here = place // 2 == 0
    ends = [jnp.where(here, pairs[0][at], pairs[1][at]) for at in (0, 1)]
    return jnp.stack(ends + [jnp.where(here, pairs[1][at], pairs[0][at]) for at in (0, 1)])


def over_line(block, steps=1):
    moves = []
    for f in range(8):
        line = f // 2
        for _ in range(steps):
            line = RING_NEXT[line]
        moves.append((f, 2 * line + f % 2))
    return lax.ppermute(block, "fsdp", moves)


def over_side(block):
    return lax.ppermute(block, "fsdp", [(f, f ^ 1) for f in range(8)])


def owner(steps, other=0):
    place = lax.axis_index("fsdp")
    return 2 * ring_behind(place // 2, steps) + (place % 2 ^ other)


def owners():
    count = lax.axis_size("fsdp")
    if count != 8:
        return jnp.arange(8, dtype=jnp.int32)
    return jnp.stack([owner(steps, other) for other in (0, 1) for steps in range(4)]).astype(jnp.int32)


class Gather:
    def __init__(self, block):
        self.blocks = [block]
        self.sides = []

    def advance(self, *gates):
        block = after(self.blocks[-1], *gates)
        moved = [over_side(block)]
        self.sides.append(moved[0])
        if len(self.sides) < 4:
            moved.append(over_line(block))
            self.blocks.append(moved[1])
        return moved

    def result(self):
        return self.blocks + self.sides


class Reduce:
    def __init__(self, blocks):
        self.blocks = blocks
        self.step = 0
        self.got = 0.0

    def advance(self, *gates):
        self.step += 1
        moved = [over_side(after(self.blocks[4 + self.step % 4], *gates))]
        if self.step > 1:
            moved.append(over_line(after(self.total.astype(BF), *gates)))
            self.got = moved[1].astype(F32)
        self.total = self.got + moved[0].astype(F32) + self.blocks[self.step % 4].astype(F32)
        return moved


def turn(rows):
    moves = []
    for f in range(8):
        for s in range(4):
            moves.append((f * 4 + s, (2 * s + f % 2) * 4 + f // 2))
    return lax.ppermute(rows, BOTH, moves)


ROWS = 256


def allowed_pairs(first_ref, row_start, key_start, width):
    key_pos = key_start + lax.broadcasted_iota(jnp.int32, (ROWS, width), 1)
    query_pos = row_start + lax.broadcasted_iota(jnp.int32, (ROWS, width), 0)
    first = first_ref[pl.ds(row_start, ROWS), :]
    return (key_pos <= query_pos) & (key_pos >= first)


def key_window(row_start):
    key_start = max(0, row_start - (MAX_DOC + ROWS - 1) // ROWS * ROWS)
    return key_start, row_start + ROWS - key_start


def dot_t(left, right):
    return lax.dot_general(left, right, (((1,), (1,)), ((), ())), preferred_element_type=F32)


def t_dot(left, right):
    return lax.dot_general(left, right, (((0,), (0,)), ((), ())), preferred_element_type=F32)


def parts_of(refs):
    return [ref.at[pl.ds(at, ROWS)] for ref in refs for at in range(0, ref.shape[0], ROWS)]


def row_starts(place_ref):
    return [pl.multiple_of((place_ref[0] ^ bits) * ROWS, ROWS) for bits in (0, 2, 1, 3)]


def put_part(sent_ref, kept_ref, part, values):
    if part < 2:
        kept_ref[part] = values.astype(BF)
    else:
        sent_ref[part - 2] = values.astype(BF)


def place_blocks(info_ref, blocks, places):
    for slot, block in enumerate(blocks):
        at = info_ref[1 + slot]
        for target, first_row, rows, cols, turned in places:
            where = (at % 2 * 4 + at // 2) if turned else at
            values = block[pl.ds(first_row, rows), pl.ds(0, cols)].astype(target.dtype)
            target[pl.ds(pl.multiple_of(where * rows, 8 if turned else 32), rows), :] = values


def attend_places(blocks, qkv_weight, out_weight):
    top, each = qkv_weight.shape[0] // 8, out_weight.shape[0] // 8
    width = out_weight.shape[1]
    return [(qkv_weight, 0, top, qkv_weight.shape[1], False), (out_weight, top, each, width, True)]


def feed_places(up_weight, down_weight):
    each, width = up_weight.shape[0] // 8, up_weight.shape[1]
    return [(up_weight, 0, each, width, False), (down_weight, each, each, width, False)]


def attend_kernel(place_ref, first_ref, *refs):
    blocks, parts = refs[:8], parts_of(refs[8:-7])
    mixed_ref, attended_ref, total_ref, sent_ref, kept_ref, qkv_weight, out_weight = refs[-7:]
    length, group = attended_ref.shape
    heads = group // HD
    scale = jnp.asarray(HD ** (-0.5), BF)
    starts = row_starts(place_ref)
    place_blocks(place_ref, blocks, attend_places(blocks, qkv_weight, out_weight))
    weight = qkv_weight[...]
    for part, start in zip(parts, starts):
        mixed_ref[pl.ds(start, ROWS), :] = jnp.dot(part[...], weight, preferred_element_type=F32).astype(BF)
    for row_start in range(0, length, ROWS):
        key_start, width = key_window(row_start)
        allowed = allowed_pairs(first_ref, row_start, key_start, width)
        outs = []
        totals = []
        for head in range(heads):
            at = head * HD
            query = mixed_ref[pl.ds(row_start, ROWS), pl.ds(at, HD)] * scale
            keys = mixed_ref[pl.ds(key_start, width), pl.ds(group + at, HD)]
            values = mixed_ref[pl.ds(key_start, width), pl.ds(2 * group + at, HD)]
            scores = jnp.where(allowed, dot_t(query, keys), MASKED)
            top = jnp.max(scores, axis=1, keepdims=True)
            weights = jnp.exp(scores - top)
            total = jnp.sum(weights, axis=1, keepdims=True)
            low = (weights * (1.0 / total)).astype(BF)
            outs.append(jnp.dot(low, values, preferred_element_type=F32))
            totals.append(top + jnp.log(total))
        attended_ref[pl.ds(row_start, ROWS), :] = jnp.concatenate(outs, axis=1).astype(BF)
        total_ref[pl.ds(row_start, ROWS), :] = jnp.concatenate(totals, axis=1)
    weight = out_weight[...].astype(BF)
    for part, start in enumerate(starts):
        values = jnp.dot(attended_ref[pl.ds(start, ROWS), :], weight, preferred_element_type=F32)
        put_part(sent_ref, kept_ref, part, values)


TAKES = {"attend": 10, "attend_back": 14, "attend_sum": 5, "feed": 5, "feed_back": 8, "feed_sum": 6}


def call(kernel, name, outs, scratch, *args):
    in_specs = [pl.BlockSpec(memory_space=pltpu.SMEM)] + [pl.BlockSpec(memory_space=pltpu.VMEM)] * (len(args) - 1)
    return pl.pallas_call(
        kernel,
        in_specs=in_specs,
        out_shape=tuple(jax.ShapeDtypeStruct(shape, dtype) for shape, dtype in outs),
        scratch_shapes=[pltpu.VMEM(shape, dtype) for shape, dtype in scratch],
        cost_estimate=pl.CostEstimate(flops=TAKES[name] * 10**9, bytes_accessed=TAKES[name] * 3 * 10**6, transcendentals=0),
        compiler_params=pltpu.CompilerParams(vmem_limit_bytes=56 << 20),
        name=name,
    )(*args)


def two_parts(width):
    return [((2, ROWS, width), BF)] * 2


def attend(place, first, blocks, parts, group):
    length, width = first.shape[0], blocks[0].shape[1]
    outs = [((length, 3 * group), BF), ((length, group), BF), ((length, group // HD), F32)] + two_parts(width)
    scratch = [((width, 3 * group), BF), ((group, width), F32)]
    return call(attend_kernel, "attend", outs, scratch, place, first, *blocks, *parts)


def attend_back_kernel(place_ref, first_ref, mixed_ref, total_ref, *refs):
    blocks, parts = refs[:8], parts_of(refs[8:-8])
    out_ref, sent_ref, kept_ref, qkv_weight, out_weight, cot_ref, key_acc, value_acc = refs[-8:]
    length, group = key_acc.shape
    heads = group // HD
    scale = jnp.asarray(HD ** (-0.5), BF)
    starts = row_starts(place_ref)
    place_blocks(place_ref, blocks, attend_places(blocks, qkv_weight, out_weight))
    weight = out_weight[...].astype(BF)
    for part, start in zip(parts, starts):
        cot_ref[pl.ds(start, ROWS), :] = dot_t(part[...], weight)
    key_acc[...] = jnp.zeros_like(key_acc)
    value_acc[...] = jnp.zeros_like(value_acc)
    for row_start in range(0, length, ROWS):
        key_start, width = key_window(row_start)
        allowed = allowed_pairs(first_ref, row_start, key_start, width)
        query_grads = []
        key_grads = []
        value_grads = []
        for head in range(heads):
            at = head * HD
            query = mixed_ref[pl.ds(row_start, ROWS), pl.ds(at, HD)] * scale
            keys = mixed_ref[pl.ds(key_start, width), pl.ds(group + at, HD)]
            values = mixed_ref[pl.ds(key_start, width), pl.ds(2 * group + at, HD)]
            cot = cot_ref[pl.ds(row_start, ROWS), pl.ds(at, HD)].astype(BF)
            total = total_ref[pl.ds(row_start, ROWS), pl.ds(head, 1)]
            scores = jnp.where(allowed, dot_t(query, keys) - total, MASKED)
            probs = jnp.exp(scores)
            prob_cot = dot_t(cot, values)
            delta = jnp.sum(probs * prob_cot, axis=1, keepdims=True)
            score_cot = (probs * (prob_cot - delta)).astype(BF)
            query_grads.append(jnp.dot(score_cot, keys, preferred_element_type=F32) * scale)
            key_grads.append(t_dot(score_cot, query))
            value_grads.append(t_dot(probs.astype(BF), cot))
        out_ref[pl.ds(row_start, ROWS), pl.ds(0, group)] = jnp.concatenate(query_grads, axis=1).astype(BF)
        window = pl.ds(key_start, width)
        key_acc[window, :] += jnp.concatenate(key_grads, axis=1)
        value_acc[window, :] += jnp.concatenate(value_grads, axis=1)
    out_ref[:, pl.ds(group, group)] = key_acc[...].astype(BF)
    out_ref[:, pl.ds(2 * group, group)] = value_acc[...].astype(BF)
    weight = qkv_weight[...]
    for part, start in enumerate(starts):
        put_part(sent_ref, kept_ref, part, dot_t(out_ref[pl.ds(start, ROWS), :], weight))


def attend_back(place, first, blocks, mixed, totals, parts):
    length, wide = mixed.shape
    group, width = wide // 3, blocks[0].shape[1]
    outs = [((length, wide), BF)] + two_parts(width)
    scratch = [((width, wide), BF), ((group, width), F32)] + [((length, group), F32)] * 3
    return call(attend_back_kernel, "attend_back", outs, scratch, place, first, mixed, totals, *blocks, *parts)


def joint(parts):
    return jnp.concatenate([part[...] for part in parts], axis=0)


def attend_sum_kernel(count, place_ref, mixed_cot_ref, attended_ref, *refs):
    normed, cots = parts_of(refs[:count]), parts_of(refs[count:-10])
    outs, qkv_grad, out_grad = refs[-10:-2], refs[-2], refs[-1]
    width, wide = qkv_grad.shape
    top, each = width // 8, out_grad.shape[0] // 8
    starts = row_starts(place_ref)
    mixed_cot = jnp.concatenate([mixed_cot_ref[pl.ds(start, ROWS), :] for start in starts], axis=0)
    qkv_grad[...] = t_dot(joint(normed), mixed_cot).astype(BF)
    attended = jnp.concatenate([attended_ref[pl.ds(start, ROWS), :] for start in starts], axis=0)
    out_grad[...] = t_dot(attended, joint(cots))
    for slot, out in enumerate(outs):
        at = place_ref[1 + slot]
        out[pl.ds(0, top), :] = jnp.zeros((top, width), BF)
        out[pl.ds(0, top), pl.ds(0, wide)] = qkv_grad[pl.ds(pl.multiple_of(at * top, 32), top), :]
        turned = pl.multiple_of((at % 2 * 4 + at // 2) * each, 8)
        out[pl.ds(top, each), :] = out_grad[pl.ds(turned, each), :].astype(BF)


def attend_sum(place, mixed_cot, attended, normed, cots):
    width, group = cots[0].shape[1], attended.shape[1]
    kernel = functools.partial(attend_sum_kernel, len(normed))
    outs = [((width // 8 + group // 8, width), BF)] * 8
    scratch = [((width, 3 * group), BF), ((group, width), F32)]
    return call(kernel, "attend_sum", outs, scratch, place, mixed_cot, attended, *normed, *cots)


def gelu_tanh(values):
    return 0.5 * values * (1.0 + jnp.tanh(0.7978845608028654 * (values + 0.044715 * values * values * values)))


def feed_kernel(place_ref, *refs):
    blocks, parts = refs[:8], parts_of(refs[8:-4])
    sent_ref, kept_ref, up, down = refs[-4:]
    place_blocks(place_ref, blocks, feed_places(up, down))
    for at, part in enumerate(parts):
        active = gelu_tanh(jnp.dot(part[...], up[...], preferred_element_type=F32)).astype(BF)
        put_part(sent_ref, kept_ref, at, jnp.dot(active, down[...], preferred_element_type=F32))


def feed_scratch(blocks):
    rows, width = blocks[0].shape
    return [((4 * rows, width), BF)] * 2


def feed(place, blocks, parts):
    return call(feed_kernel, "feed", two_parts(blocks[0].shape[1]), feed_scratch(blocks), place, *blocks, *parts)


def feed_back_kernel(place_ref, *refs):
    blocks, refs, (active_ref, cot_ref, sent_ref, kept_ref, up, down) = refs[:8], refs[8:-6], refs[-6:]
    normed, cots = parts_of(refs[: len(refs) // 2]), parts_of(refs[len(refs) // 2 :])
    place_blocks(place_ref, blocks, feed_places(up, down))
    for at, (part, cot) in enumerate(zip(normed, cots)):
        upper = jnp.dot(part[...], up[...], preferred_element_type=F32)
        square = upper * upper
        bent = jnp.tanh(0.7978845608028654 * (upper + 0.044715 * upper * square))
        inner = 0.7978845608028654 * (1.0 + 3.0 * 0.044715 * square)
        half_up = 0.5 * upper
        rows = pl.ds(at * ROWS, ROWS)
        active_ref[rows, :] = (half_up * (1.0 + bent)).astype(BF)
        slope = 0.5 * (1.0 + bent) + half_up * (1.0 - bent * bent) * inner
        upper_cot = (slope * dot_t(cot[...], down[...])).astype(BF)
        cot_ref[rows, :] = upper_cot
        put_part(sent_ref, kept_ref, at, dot_t(upper_cot, up[...]))


def feed_back(place, blocks, normed, cots):
    rows, width = blocks[0].shape
    outs = [((4 * ROWS, 4 * rows), BF)] * 2 + two_parts(width)
    return call(feed_back_kernel, "feed_back", outs, feed_scratch(blocks), place, *blocks, *normed, *cots)


def feed_sum_kernel(place_ref, active_ref, upper_cot_ref, *refs):
    outs, up_grad, down_grad = refs[-10:-2], refs[-2], refs[-1]
    refs = refs[:-10]
    normed, cots = parts_of(refs[: len(refs) // 2]), parts_of(refs[len(refs) // 2 :])
    each = up_grad.shape[0] // 8
    up_grad[...] = t_dot(joint(normed), upper_cot_ref[...]).astype(BF)
    down_grad[...] = t_dot(active_ref[...], joint(cots)).astype(BF)
    for slot, out in enumerate(outs):
        rows = pl.ds(pl.multiple_of(place_ref[1 + slot] * each, 32), each)
        out[pl.ds(0, each), :] = up_grad[rows, :]
        out[pl.ds(each, each), :] = down_grad[rows, :]


def feed_sum(place, active, upper_cot, normed, cots):
    width, inner = cots[0].shape[1], active.shape[1]
    outs = [((inner // 4, width), BF)] * 8
    scratch = [((width, inner), BF), ((inner, width), BF)]
    return call(feed_sum_kernel, "feed_sum", outs, scratch, place, active, upper_cot, *normed, *cots)


def store_kernel(fsdp, *refs):
    qkv_out, out_out, up_out, down_out = refs[6:]
    for layer in range(LAYERS):
        columns_ref, rows_ref, fed_ref = refs[3 * layer : 3 * layer + 3]
        out_out[layer] = rows_ref[...].astype(F32)
        down_out[layer] = fed_ref[pl.ds(fed_ref.shape[0] - down_out.shape[1], down_out.shape[1]), :]
        seq = columns_ref.shape[0]
        inner, group = up_out.shape[2] // seq, qkv_out.shape[2] // (3 * seq)
        for quarter in range(seq):
            values = columns_ref[quarter].astype(F32)
            each = inner // fsdp
            for part in range(fsdp):
                at = (part * seq + quarter) * each
                up_out[layer, :, pl.ds(at, each)] = values[:, part * each : part * each + each]
            for part in range(3):
                at = (part * seq + quarter) * group
                start = inner + part * group
                qkv_out[layer, :, pl.ds(at, group)] = values[:, start : start + group]


def store(sent_0, sent_1, group, seq, fsdp):
    piece, width = sent_0[1].shape
    inner = sent_0[0].shape[2] - 3 * group
    shapes = [(piece, 3 * group * seq), (piece, width), (piece, inner * seq), (inner * seq // (fsdp * seq), width)]
    outs = [((LAYERS,) + shape, F32) for shape in shapes]
    args = sent_0 + sent_1
    return pl.pallas_call(
        functools.partial(store_kernel, fsdp),
        out_shape=tuple(jax.ShapeDtypeStruct(shape, dtype) for shape, dtype in outs),
        compiler_params=pltpu.CompilerParams(vmem_limit_bytes=56 << 20),
        name="store",
    )(*args)


def norm_parts(values):
    center = values - jnp.mean(values, axis=-1, keepdims=True)
    inverse = lax.rsqrt(jnp.mean(center * center, axis=-1, keepdims=True) + NORM_EPS)
    return center * inverse, inverse


def norm_back(unit, inverse, gain, cot):
    scaled = cot * gain
    inner = scaled - jnp.mean(scaled, axis=-1, keepdims=True)
    inner = inner - unit * jnp.mean(scaled * unit, axis=-1, keepdims=True)
    return inner * inverse, jnp.sum(cot * unit, axis=0), jnp.sum(cot, axis=0)


NORM_AT = 640


def norm_kernel(place_ref, *refs):
    blocks, out_ref, both = refs[:8], refs[8], refs[9]
    each = both.shape[0] // 8
    for slot, block in enumerate(blocks):
        both[pl.ds(pl.multiple_of(place_ref[1 + slot] * each, 32), each), :] = block[...].astype(F32)
    out_ref[...] = both[...].T[:8]


def norms_of(place, blocks):
    width = blocks[0].shape[1]
    part = pl.BlockSpec((width // 8, 128), lambda step: (0, NORM_AT // 128))
    return pl.pallas_call(
        norm_kernel,
        grid=(1,),
        in_specs=[pl.BlockSpec(memory_space=pltpu.SMEM)] + [part] * 8,
        out_shape=jax.ShapeDtypeStruct((8, width), F32),
        scratch_shapes=[pltpu.VMEM((width, 128), F32)],
        name="norms_of",
    )(place, *blocks)


def shards(tokens, norm_gains, norm_shifts, w_qkv, w_out, w_up, w_down, out_grad, doc_lengths):
    tok_rows, width = tokens.shape
    fsdp, seq = lax.axis_size("fsdp"), lax.axis_size("seq")
    ruled = fsdp == 8
    length = tok_rows * seq
    group = (H // seq) * HD
    piece = w_qkv.shape[1]
    inner = w_up.shape[2] // seq
    unit_rows = w_down.shape[1]
    place = lax.axis_index("seq")

    ends = jnp.cumsum(doc_lengths[0])
    starts = ends - doc_lengths[0]
    positions = lax.iota(jnp.int32, length)
    first = jnp.max(jnp.where(positions[:, None] >= starts[None, :], starts[None, :], 0), axis=1, keepdims=True)

    def column_parts(layer):
        qkv = w_qkv[layer].astype(BF).reshape(piece, 3, seq, group).transpose(2, 0, 1, 3)
        up = w_up[layer].astype(BF).reshape(piece, fsdp, seq, unit_rows).transpose(2, 0, 1, 3)
        return qkv.reshape(seq, piece, 3 * group), up.reshape(seq, piece, inner)

    def pad_cols(values, cols):
        return jnp.pad(values, [(0, 0)] * (values.ndim - 1) + [(0, cols - values.shape[-1])])

    place_ref = jnp.concatenate([place.reshape(1).astype(jnp.int32), owners()])
    norms = jnp.stack([norm_gains, norm_shifts]).astype(BF).reshape(8, piece).T
    norms = jnp.pad(norms, ((0, 0), (NORM_AT - 3 * group, width - NORM_AT - 8)))
    qkv_parts = [None, None]
    up_parts = [None, None]
    for layer in range(LAYERS):
        qkv_parts[layer], up_parts[layer] = column_parts(layer)
    early = jnp.concatenate([qkv_parts[0], jnp.broadcast_to(norms[None], (seq,) + norms.shape)], axis=2)
    early = exchange_seq(early).reshape(seq * piece, width)
    attn_low = [None, None]
    feed_low = [None, None]

    def wide_blocks(values):
        return pad_cols(values.reshape(8, -1, values.shape[-1]), width)

    def out_blocks(rows):
        return rows.reshape(2, 4, -1, width).transpose(1, 0, 2, 3).reshape(8, -1, width)

    def out_rows_of(blocks):
        return blocks.reshape(4, 2, -1, width).transpose(1, 0, 2, 3).reshape(-1, width)

    if ruled:
        out_rows = turn(w_out.astype(BF))
        early = jnp.concatenate([early, out_rows[0]])
        mark = [early]
        first_gather = Gather(early)
        first_moved = first_gather.advance()
    else:
        mark = []
        first_steps = []
    all_tokens = gather_seq(after(tokens, *mark))
    later = jnp.concatenate([up_parts[0], pad_cols(qkv_parts[1], inner), up_parts[1]], axis=1)
    later = exchange_seq(after(later, *mark))
    up_first = later[:, :piece].reshape(seq * piece, inner)
    qkv_next = later[:, piece : 2 * piece].reshape(seq * piece, inner)
    up_next = later[:, 2 * piece :].reshape(seq * piece, inner)
    if ruled:
        first_moved = first_gather.advance(*first_moved)
        low_down = w_down.astype(BF)
        feed_gather = [
            Gather(jnp.concatenate([up_first, low_down[0]])),
            Gather(jnp.concatenate([up_next, low_down[1]])),
        ]
        attn_gather = Gather(jnp.concatenate([qkv_next, out_rows[1]]))
        first_gather.advance(feed_gather[0].blocks[0], *first_moved)
        moved = feed_gather[0].advance(*first_moved)
        first_gather.advance(first_gather.sides[2])
        first_steps = feed_gather[0].advance(first_gather.blocks[3], *moved)
        attn_low[0] = first_gather.result()
    else:
        early = lax.all_gather(early, "fsdp", axis=0, tiled=True)

        def gathered(columns):
            return lax.all_gather(columns, "fsdp", axis=0, tiled=True)

        def attn_joined(columns, rows):
            rows = lax.all_gather(rows.astype(BF), BOTH, axis=0, tiled=True)
            rows = lax.dynamic_slice_in_dim(rows, place * group, group, 0)
            return jnp.concatenate([columns.reshape(8, -1, width), out_blocks(rows)], axis=1)

        attn_low = [list(attn_joined(early, w_out[0])), list(attn_joined(gathered(qkv_next), w_out[1]))]
        for layer, columns in enumerate((up_first, up_next)):
            blocks = gathered(columns), gathered(w_down[layer].astype(BF))
            feed_low[layer] = list(jnp.concatenate([wide_blocks(part) for part in blocks], axis=1))

    norm_low = norms_of(place_ref, attn_low[0]).reshape(2, LAYERS, 2, width)
    gains, shifts = norm_low[0], norm_low[1]

    plan = {}
    if ruled:
        plan = {
            ("scatter_a", 0): [feed_gather[0], attn_gather],
            ("gather_b", 0): [feed_gather[0], attn_gather],
            ("scatter_b", 0): [attn_gather, feed_gather[1]],
            ("gather_a", 1): [attn_gather, feed_gather[1]],
            ("scatter_a", 1): [feed_gather[1]],
            ("gather_b", 1): [feed_gather[1]],
        }

    def steps(what, layer):
        def work(gate):
            return sum([each.advance(gate) for each in plan.get((what, layer), [])], [])

        return work

    def beside_main(value, what, layer):
        moved = steps(what, layer)(value)
        return after(value, *moved)

    first_cot = gather_seq(after((BRANCH_SCALE * out_grad.astype(F32)).astype(BF), all_tokens[1]))
    first_steps = first_steps + first_cot[1:]

    hidden = tokens.astype(F32)
    saved = []
    for layer in range(LAYERS):
        unit_a, inverse_a = norm_parts(hidden)
        if layer == 0:
            normed_a = (norm_parts(jnp.concatenate(all_tokens).astype(F32))[0] * gains[0, 0] + shifts[0, 0]).astype(BF)
            normed_a = [after(normed_a, *first_steps)]
        else:
            normed_a = (unit_a * gains[layer, 0] + shifts[layer, 0]).astype(BF)
            normed_a = gather_seq(normed_a, steps("gather_a", layer))
        normed_a[-1] = beside_main(normed_a[-1], "normed_a", layer)
        if ruled and layer > 0:
            attn_low[layer] = attn_gather.result()
        mixed, attended, totals, sent, kept = attend(place_ref, first, attn_low[layer], normed_a, group)
        sent = beside_main(sent, "attended", layer)
        hidden = hidden + BRANCH_SCALE * scatter_seq(sent, kept, steps("scatter_a", layer))
        unit_b, inverse_b = norm_parts(hidden)
        normed_b = (unit_b * gains[layer, 1] + shifts[layer, 1]).astype(BF)
        normed_b = gather_seq(normed_b, steps("gather_b", layer))
        normed_b[-1] = beside_main(normed_b[-1], "normed_b", layer)
        if ruled:
            feed_low[layer] = feed_gather[layer].result()
        if layer < LAYERS - 1:
            sent, kept = feed(place_ref, feed_low[layer], normed_b)
            hidden = hidden + BRANCH_SCALE * scatter_seq(sent, kept, steps("scatter_b", layer))
        saved.append((unit_a, inverse_a, normed_a, mixed, attended, totals, unit_b, inverse_b, normed_b))
    last_feed = []

    cot = out_grad.astype(F32)
    norm_sums = []
    sums_of = {}
    grads_of = {}

    def start_sum(name, blocks):
        if ruled:
            sums_of[name] = Reduce(blocks)
        else:
            grads_of[name] = jnp.stack(blocks)
        return [blocks[0]]

    def step_sums(gate, *names):
        return sum([sums_of[name].advance(gate) for name in names], []) if ruled else []

    back_plan = {
        ("gather_a", 1): [("feed", 1)],
        ("scatter_a", 1): [("feed", 1)],
        ("gather_b", 0): [("feed", 1), ("attn", 1)],
        ("scatter_b", 0): [("feed", 1), ("attn", 1)],
        ("gather_a", 0): [("feed", 0), ("attn", 1)],
        ("scatter_a", 0): [("feed", 0), ("attn", 1)],
        ("after_sum", 0): [("attn", 0)],
    }
    for layer in reversed(range(LAYERS)):
        unit_a, inverse_a, normed_a, mixed, attended, totals, unit_b, inverse_b, normed_b = saved[layer]

        def sum_steps(what):
            return lambda gate: step_sums(gate, *back_plan.get((what, layer), []))

        if layer == LAYERS - 1:
            down_cot = first_cot
        else:
            down_cot = gather_seq((BRANCH_SCALE * cot).astype(BF), sum_steps("gather_b"))
        active, upper_cot, sent, kept = feed_back(place_ref, feed_low[layer], normed_b, down_cot)

        def feed_work(gate):
            moved = start_sum(("feed", layer), feed_sum(place_ref, after(active, gate), upper_cot, normed_b, down_cot))
            return moved + sum_steps("scatter_b")(gate)

        second_cot = scatter_seq(sent, kept, feed_work)
        back, gain_sum_b, shift_sum_b = norm_back(unit_b, inverse_b, gains[layer, 1], second_cot)
        cot = cot + back

        def norm_work(gate):
            if layer == LAYERS - 1:
                parts = [after(normed_b[0], gate)] + normed_b[1:]
                last_feed.extend(feed(place_ref, feed_low[layer], parts))
            return sum_steps("gather_a")(gate) + last_feed[:1]

        attn_cot = gather_seq((BRANCH_SCALE * cot).astype(BF), norm_work)
        mixed_cot, sent, kept = attend_back(place_ref, first, attn_low[layer], mixed, totals, attn_cot)
        sent = after(sent, *sum_steps("back")(mixed_cot))

        def attn_work(gate):
            joined = attend_sum(place_ref, after(mixed_cot, gate), attended, normed_a, attn_cot)
            moved = sum_steps("scatter_a")(gate) + start_sum(("attn", layer), joined)
            return moved + sum_steps("after_sum")(gate)

        normed_cot = scatter_seq(sent, kept, attn_work)
        back, gain_sum_a, shift_sum_a = norm_back(unit_a, inverse_a, gains[layer, 0], normed_cot)
        cot = cot + back
        norm_sums.append(jnp.concatenate([gain_sum_a, gain_sum_b, shift_sum_a, shift_sum_b]))

    sent, kept = last_feed
    sums = jnp.concatenate(norm_sums[::-1])
    column_back = {}
    row_back = {}

    def send_home(layer, *gates):
        attn, fed = sums_of["attn", layer].total, sums_of["feed", layer].total
        columns = jnp.concatenate([fed[: seq * piece], attn[: seq * piece, : 3 * group]], axis=1).astype(BF)
        rows = after(attn[seq * piece :].astype(BF), *gates)
        columns = exchange_seq(after(columns, *gates).reshape(seq, piece, -1))
        return columns, turn(rows), fed

    def take(layer):
        def summed(blocks):
            return lax.psum_scatter(blocks, "fsdp", scatter_dimension=0, tiled=True).astype(F32)

        joined = grads_of["attn", layer]
        column_back["qkv", layer] = summed(joined[:, : width // 8, : 3 * group].reshape(width, 3 * group))
        rows = out_rows_of(joined[:, width // 8 :])
        spread = jnp.zeros((seq,) + rows.shape, BF)
        spread = lax.dynamic_update_index_in_dim(spread, rows, place, 0).reshape(-1, width)
        row_back["out", layer] = lax.psum_scatter(spread, BOTH, scatter_dimension=0, tiled=True).astype(F32)
        joined = grads_of["feed", layer]
        column_back["up", layer] = summed(joined[:, : width // 8].reshape(width, inner))
        row_back["down", layer] = summed(joined[:, width // 8 :].reshape(inner, width))

    def home(layer):
        both = jnp.concatenate([column_back["up", layer], column_back["qkv", layer]], axis=1).astype(BF)
        both = exchange_seq(both.reshape(seq, piece, -1)).astype(F32)
        qkv = both[:, :, inner:].reshape(seq, piece, 3, group).transpose(1, 2, 0, 3).reshape(piece, -1)
        up = both[:, :, :inner].reshape(seq, piece, fsdp, unit_rows).transpose(1, 2, 0, 3)
        return up.reshape(piece, -1), qkv

    if ruled:
        mark = sums_of["attn", 0].advance() + sums_of["feed", 0].advance()
        near = swap_seq(after(sent, cot), 1)
        sums = after(sums + swap_seq(sums, 1), *mark, near)
        half = kept.astype(F32) + near.astype(F32)
        mark = step_sums(sums, ("attn", 0), ("feed", 0))
        got = swap_seq(after(half[1].astype(BF), sums), 2)
        sums = after(sums + swap_seq(sums, 2), *mark, got)
        mark = step_sums(sums, ("attn", 0))
        sums = after(sums + lax.ppermute(sums, "fsdp", [(f, f ^ 1) for f in range(8)]), *mark)
        outputs = hidden + BRANCH_SCALE * (half[0] + got.astype(F32))
        sent_1 = send_home(1, sums)
        for bit in (2, 4):
            sums = sums + lax.ppermute(sums, "fsdp", [(f, f ^ bit) for f in range(8)])
        weight_grads = store(send_home(0), sent_1, group, seq, fsdp)
    else:
        take(0)
        take(1)
        outputs = hidden + BRANCH_SCALE * scatter_seq(sent, kept)
        home_0, home_1 = home(0), home(1)
        sums = lax.psum(sums, BOTH)
        up_grads, qkv_grads = zip(home_0, home_1)
        out_grads = [row_back["out", layer] for layer in range(LAYERS)]
        down_grads = [row_back["down", layer] for layer in range(LAYERS)]
        weight_grads = [jnp.stack(grads) for grads in (qkv_grads, out_grads, up_grads, down_grads)]
    whose = lax.axis_index("fsdp") * seq + place
    sums = lax.dynamic_slice_in_dim(sums.reshape(-1, width), whose * piece, piece, 1).reshape(LAYERS, 4, piece)
    return (
        outputs.astype(BF),
        cot.astype(BF),
        sums[:, :2],
        sums[:, 2],
        sums[:, 3],
        *weight_grads,
    )


def solution(mesh):
    rows = P(BOTH, None)
    thirds = P(None, None, BOTH)
    middle = P(None, BOTH, None)
    return jax.shard_map(
        shards,
        mesh=mesh,
        in_specs=(rows, thirds, thirds, middle, middle, middle, middle, rows, P("fsdp", None)),
        out_specs=(rows, rows, thirds, P(None, BOTH), P(None, BOTH), middle, middle, middle, middle),
        check_vma=False,
    )
```

```python
import functools

import jax
import jax.numpy as jnp
from jax import lax
from jax.experimental import pallas as pl
from jax.experimental.pallas import tpu as pltpu
from jax.sharding import PartitionSpec as P

H = 12
HD = 64
LAYERS = 2
MAX_DOC = 512

NORM_EPS = 1e-05
BRANCH_SCALE = 0.7071067811865476
MASKED = -1e30
BF = jnp.bfloat16
F32 = jnp.float32
BOTH = ("fsdp", "seq")

RING_NEXT = (1, 3, 0, 2)


def ring_behind(line, steps):
    at = ((line ^ (line >> 1)) - steps) & 3
    return at ^ (at >> 1)


def after(value, *others):
    return lax.optimization_barrier((value,) + others)[0] if others else value


def swap_seq(values, bit):
    return lax.ppermute(values, "seq", [(s, s ^ bit) for s in range(4)])


def by_bit(bit, own, other):
    zero = bit == 0
    return jnp.where(zero, own, other), jnp.where(zero, other, own)


def gather_seq(rows, work=None):
    far = swap_seq(rows, 2)
    near = swap_seq(rows, 1)
    if work is not None:
        far = after(far, *work(rows))
    return [rows, far, near, swap_seq(far, 1)]


def scatter_seq(sent, kept, work=None):
    half = kept.astype(F32) + swap_seq(sent, 1).astype(F32)
    sent = half[1].astype(BF)
    got = swap_seq(sent, 2)
    if work is not None:
        got = after(got, *work(sent))
    return half[0] + got.astype(F32)


def exchange_seq(parts):
    place = lax.axis_index("seq")
    own = [lax.dynamic_index_in_dim(parts, place ^ bits, 0, keepdims=False) for bits in range(4)]
    got = own[:1] + [swap_seq(own[bits], bits) for bits in (1, 2, 3)]
    core = place % 2 == 0
    pairs = [(jnp.where(core, got[at], got[at + 1]), jnp.where(core, got[at + 1], got[at])) for at in (0, 2)]
    here = place // 2 == 0
    ends = [jnp.where(here, pairs[0][at], pairs[1][at]) for at in (0, 1)]
    return jnp.stack(ends + [jnp.where(here, pairs[1][at], pairs[0][at]) for at in (0, 1)])


def over_line(block, steps=1):
    moves = []
    for f in range(8):
        line = f // 2
        for _ in range(steps):
            line = RING_NEXT[line]
        moves.append((f, 2 * line + f % 2))
    return lax.ppermute(block, "fsdp", moves)


def over_side(block):
    return lax.ppermute(block, "fsdp", [(f, f ^ 1) for f in range(8)])


def owner(steps, other=0):
    place = lax.axis_index("fsdp")
    return 2 * ring_behind(place // 2, steps) + (place % 2 ^ other)


def owners():
    count = lax.axis_size("fsdp")
    if count != 8:
        return jnp.arange(8, dtype=jnp.int32)
    return jnp.stack([owner(steps, other) for other in (0, 1) for steps in range(4)]).astype(jnp.int32)


class Gather:
    def __init__(self, block):
        self.blocks = [block]
        self.sides = []

    def advance(self, *gates):
        block = after(self.blocks[-1], *gates)
        moved = [over_side(block)]
        self.sides.append(moved[0])
        if len(self.sides) < 4:
            moved.append(over_line(block))
            self.blocks.append(moved[1])
        return moved

    def result(self):
        return self.blocks + self.sides


class Reduce:
    def __init__(self, blocks):
        self.blocks = blocks
        self.step = 0
        self.got = 0.0

    def advance(self, *gates):
        self.step += 1
        moved = [over_side(after(self.blocks[4 + self.step % 4], *gates))]
        if self.step > 1:
            moved.append(over_line(after(self.total.astype(BF), *gates)))
            self.got = moved[1].astype(F32)
        self.total = self.got + moved[0].astype(F32) + self.blocks[self.step % 4].astype(F32)
        return moved


def turn(rows):
    moves = []
    for f in range(8):
        for s in range(4):
            moves.append((f * 4 + s, (2 * s + f % 2) * 4 + f // 2))
    return lax.ppermute(rows, BOTH, moves)


ROWS = 256


def allowed_pairs(first_ref, row_start, key_start, width):
    key_pos = key_start + lax.broadcasted_iota(jnp.int32, (ROWS, width), 1)
    query_pos = row_start + lax.broadcasted_iota(jnp.int32, (ROWS, width), 0)
    first = first_ref[pl.ds(row_start, ROWS), :]
    return (key_pos <= query_pos) & (key_pos >= first)


def key_window(row_start):
    key_start = max(0, row_start - (MAX_DOC + ROWS - 1) // ROWS * ROWS)
    return key_start, row_start + ROWS - key_start


def dot_t(left, right):
    return lax.dot_general(left, right, (((1,), (1,)), ((), ())), preferred_element_type=F32)


def t_dot(left, right):
    return lax.dot_general(left, right, (((0,), (0,)), ((), ())), preferred_element_type=F32)


def parts_of(refs):
    return [ref.at[pl.ds(at, ROWS)] for ref in refs for at in range(0, ref.shape[0], ROWS)]


def row_starts(place_ref):
    return [pl.multiple_of((place_ref[0] ^ bits) * ROWS, ROWS) for bits in (0, 2, 1, 3)]


def put_part(sent_ref, kept_ref, part, values):
    if part < 2:
        kept_ref[part] = values.astype(BF)
    else:
        sent_ref[part - 2] = values.astype(BF)


def place_blocks(info_ref, blocks, places):
    for slot, block in enumerate(blocks):
        at = info_ref[1 + slot]
        for target, first_row, rows, cols, turned in places:
            where = (at % 2 * 4 + at // 2) if turned else at
            values = block[pl.ds(first_row, rows), pl.ds(0, cols)].astype(target.dtype)
            target[pl.ds(pl.multiple_of(where * rows, 8 if turned else 32), rows), :] = values


def attend_places(blocks, qkv_weight, out_weight):
    top, each = qkv_weight.shape[0] // 8, out_weight.shape[0] // 8
    width = out_weight.shape[1]
    return [(qkv_weight, 0, top, qkv_weight.shape[1], False), (out_weight, top, each, width, True)]


def feed_places(up_weight, down_weight):
    each, width = up_weight.shape[0] // 8, up_weight.shape[1]
    return [(up_weight, 0, each, width, False), (down_weight, each, each, width, False)]


def attend_kernel(place_ref, first_ref, *refs):
    blocks, parts = refs[:8], parts_of(refs[8:-7])
    mixed_ref, attended_ref, total_ref, sent_ref, kept_ref, qkv_weight, out_weight = refs[-7:]
    length, group = attended_ref.shape
    heads = group // HD
    scale = jnp.asarray(HD ** (-0.5), BF)
    starts = row_starts(place_ref)
    place_blocks(place_ref, blocks, attend_places(blocks, qkv_weight, out_weight))
    weight = qkv_weight[...]
    for part, start in zip(parts, starts):
        mixed_ref[pl.ds(start, ROWS), :] = jnp.dot(part[...], weight, preferred_element_type=F32).astype(BF)
    for row_start in range(0, length, ROWS):
        key_start, width = key_window(row_start)
        allowed = allowed_pairs(first_ref, row_start, key_start, width)
        outs = []
        totals = []
        for head in range(heads):
            at = head * HD
            query = mixed_ref[pl.ds(row_start, ROWS), pl.ds(at, HD)] * scale
            keys = mixed_ref[pl.ds(key_start, width), pl.ds(group + at, HD)]
            values = mixed_ref[pl.ds(key_start, width), pl.ds(2 * group + at, HD)]
            scores = jnp.where(allowed, dot_t(query, keys), MASKED)
            top = jnp.max(scores, axis=1, keepdims=True)
            weights = jnp.exp(scores - top)
            total = jnp.sum(weights, axis=1, keepdims=True)
            low = (weights * (1.0 / total)).astype(BF)
            outs.append(jnp.dot(low, values, preferred_element_type=F32))
            totals.append(top + jnp.log(total))
        attended_ref[pl.ds(row_start, ROWS), :] = jnp.concatenate(outs, axis=1).astype(BF)
        total_ref[pl.ds(row_start, ROWS), :] = jnp.concatenate(totals, axis=1)
    weight = out_weight[...].astype(BF)
    for part, start in enumerate(starts):
        values = jnp.dot(attended_ref[pl.ds(start, ROWS), :], weight, preferred_element_type=F32)
        put_part(sent_ref, kept_ref, part, values)


TAKES = {"attend": 10, "attend_back": 14, "attend_sum": 5, "feed": 5, "feed_back": 8, "feed_sum": 6}


def call(kernel, name, outs, scratch, *args):
    in_specs = [pl.BlockSpec(memory_space=pltpu.SMEM)] + [pl.BlockSpec(memory_space=pltpu.VMEM)] * (len(args) - 1)
    return pl.pallas_call(
        kernel,
        in_specs=in_specs,
        out_shape=tuple(jax.ShapeDtypeStruct(shape, dtype) for shape, dtype in outs),
        scratch_shapes=[pltpu.VMEM(shape, dtype) for shape, dtype in scratch],
        cost_estimate=pl.CostEstimate(flops=TAKES[name] * 10**9, bytes_accessed=TAKES[name] * 3 * 10**6, transcendentals=0),
        compiler_params=pltpu.CompilerParams(vmem_limit_bytes=56 << 20),
        name=name,
    )(*args)


def two_parts(width):
    return [((2, ROWS, width), BF)] * 2


def attend(place, first, blocks, parts, group):
    length, width = first.shape[0], blocks[0].shape[1]
    outs = [((length, 3 * group), BF), ((length, group), BF), ((length, group // HD), F32)] + two_parts(width)
    scratch = [((width, 3 * group), BF), ((group, width), F32)]
    return call(attend_kernel, "attend", outs, scratch, place, first, *blocks, *parts)


def attend_back_kernel(place_ref, first_ref, mixed_ref, total_ref, *refs):
    blocks, parts = refs[:8], parts_of(refs[8:-8])
    out_ref, sent_ref, kept_ref, qkv_weight, out_weight, cot_ref, key_acc, value_acc = refs[-8:]
    length, group = key_acc.shape
    heads = group // HD
    scale = jnp.asarray(HD ** (-0.5), BF)
    starts = row_starts(place_ref)
    place_blocks(place_ref, blocks, attend_places(blocks, qkv_weight, out_weight))
    weight = out_weight[...].astype(BF)
    for part, start in zip(parts, starts):
        cot_ref[pl.ds(start, ROWS), :] = dot_t(part[...], weight)
    key_acc[...] = jnp.zeros_like(key_acc)
    value_acc[...] = jnp.zeros_like(value_acc)
    for row_start in range(0, length, ROWS):
        key_start, width = key_window(row_start)
        allowed = allowed_pairs(first_ref, row_start, key_start, width)
        query_grads = []
        key_grads = []
        value_grads = []
        for head in range(heads):
            at = head * HD
            query = mixed_ref[pl.ds(row_start, ROWS), pl.ds(at, HD)] * scale
            keys = mixed_ref[pl.ds(key_start, width), pl.ds(group + at, HD)]
            values = mixed_ref[pl.ds(key_start, width), pl.ds(2 * group + at, HD)]
            cot = cot_ref[pl.ds(row_start, ROWS), pl.ds(at, HD)].astype(BF)
            total = total_ref[pl.ds(row_start, ROWS), pl.ds(head, 1)]
            scores = jnp.where(allowed, dot_t(query, keys) - total, MASKED)
            probs = jnp.exp(scores)
            prob_cot = dot_t(cot, values)
            delta = jnp.sum(probs * prob_cot, axis=1, keepdims=True)
            score_cot = (probs * (prob_cot - delta)).astype(BF)
            query_grads.append(jnp.dot(score_cot, keys, preferred_element_type=F32) * scale)
            key_grads.append(t_dot(score_cot, query))
            value_grads.append(t_dot(probs.astype(BF), cot))
        out_ref[pl.ds(row_start, ROWS), pl.ds(0, group)] = jnp.concatenate(query_grads, axis=1).astype(BF)
        window = pl.ds(key_start, width)
        key_acc[window, :] += jnp.concatenate(key_grads, axis=1)
        value_acc[window, :] += jnp.concatenate(value_grads, axis=1)
    out_ref[:, pl.ds(group, group)] = key_acc[...].astype(BF)
    out_ref[:, pl.ds(2 * group, group)] = value_acc[...].astype(BF)
    weight = qkv_weight[...]
    for part, start in enumerate(starts):
        put_part(sent_ref, kept_ref, part, dot_t(out_ref[pl.ds(start, ROWS), :], weight))


def attend_back(place, first, blocks, mixed, totals, parts):
    length, wide = mixed.shape
    group, width = wide // 3, blocks[0].shape[1]
    outs = [((length, wide), BF)] + two_parts(width)
    scratch = [((width, wide), BF), ((group, width), F32)] + [((length, group), F32)] * 3
    return call(attend_back_kernel, "attend_back", outs, scratch, place, first, mixed, totals, *blocks, *parts)


def joint(parts):
    return jnp.concatenate([part[...] for part in parts], axis=0)


def attend_sum_kernel(count, place_ref, mixed_cot_ref, attended_ref, *refs):
    normed, cots = parts_of(refs[:count]), parts_of(refs[count:-10])
    outs, qkv_grad, out_grad = refs[-10:-2], refs[-2], refs[-1]
    width, wide = qkv_grad.shape
    top, each = width // 8, out_grad.shape[0] // 8
    starts = row_starts(place_ref)
    mixed_cot = jnp.concatenate([mixed_cot_ref[pl.ds(start, ROWS), :] for start in starts], axis=0)
    qkv_grad[...] = t_dot(joint(normed), mixed_cot).astype(BF)
    attended = jnp.concatenate([attended_ref[pl.ds(start, ROWS), :] for start in starts], axis=0)
    out_grad[...] = t_dot(attended, joint(cots))
    for slot, out in enumerate(outs):
        at = place_ref[1 + slot]
        out[pl.ds(0, top), :] = jnp.zeros((top, width), BF)
        out[pl.ds(0, top), pl.ds(0, wide)] = qkv_grad[pl.ds(pl.multiple_of(at * top, 32), top), :]
        turned = pl.multiple_of((at % 2 * 4 + at // 2) * each, 8)
        out[pl.ds(top, each), :] = out_grad[pl.ds(turned, each), :].astype(BF)


def attend_sum(place, mixed_cot, attended, normed, cots):
    width, group = cots[0].shape[1], attended.shape[1]
    kernel = functools.partial(attend_sum_kernel, len(normed))
    outs = [((width // 8 + group // 8, width), BF)] * 8
    scratch = [((width, 3 * group), BF), ((group, width), F32)]
    return call(kernel, "attend_sum", outs, scratch, place, mixed_cot, attended, *normed, *cots)


def gelu_tanh(values):
    return 0.5 * values * (1.0 + jnp.tanh(0.7978845608028654 * (values + 0.044715 * values * values * values)))


def feed_kernel(place_ref, *refs):
    blocks, parts = refs[:8], parts_of(refs[8:-4])
    sent_ref, kept_ref, up, down = refs[-4:]
    place_blocks(place_ref, blocks, feed_places(up, down))
    for at, part in enumerate(parts):
        active = gelu_tanh(jnp.dot(part[...], up[...], preferred_element_type=F32)).astype(BF)
        put_part(sent_ref, kept_ref, at, jnp.dot(active, down[...], preferred_element_type=F32))


def feed_scratch(blocks):
    rows, width = blocks[0].shape
    return [((4 * rows, width), BF)] * 2


def feed(place, blocks, parts):
    return call(feed_kernel, "feed", two_parts(blocks[0].shape[1]), feed_scratch(blocks), place, *blocks, *parts)


def feed_back_kernel(place_ref, *refs):
    blocks, refs, (active_ref, cot_ref, sent_ref, kept_ref, up, down) = refs[:8], refs[8:-6], refs[-6:]
    normed, cots = parts_of(refs[: len(refs) // 2]), parts_of(refs[len(refs) // 2 :])
    place_blocks(place_ref, blocks, feed_places(up, down))
    for at, (part, cot) in enumerate(zip(normed, cots)):
        upper = jnp.dot(part[...], up[...], preferred_element_type=F32)
        square = upper * upper
        bent = jnp.tanh(0.7978845608028654 * (upper + 0.044715 * upper * square))
        inner = 0.7978845608028654 * (1.0 + 3.0 * 0.044715 * square)
        half_up = 0.5 * upper
        rows = pl.ds(at * ROWS, ROWS)
        active_ref[rows, :] = (half_up * (1.0 + bent)).astype(BF)
        slope = 0.5 * (1.0 + bent) + half_up * (1.0 - bent * bent) * inner
        upper_cot = (slope * dot_t(cot[...], down[...])).astype(BF)
        cot_ref[rows, :] = upper_cot
        put_part(sent_ref, kept_ref, at, dot_t(upper_cot, up[...]))


def feed_back(place, blocks, normed, cots):
    rows, width = blocks[0].shape
    outs = [((4 * ROWS, 4 * rows), BF)] * 2 + two_parts(width)
    return call(feed_back_kernel, "feed_back", outs, feed_scratch(blocks), place, *blocks, *normed, *cots)


def feed_sum_kernel(place_ref, active_ref, upper_cot_ref, *refs):
    outs, up_grad, down_grad = refs[-10:-2], refs[-2], refs[-1]
    refs = refs[:-10]
    normed, cots = parts_of(refs[: len(refs) // 2]), parts_of(refs[len(refs) // 2 :])
    each = up_grad.shape[0] // 8
    up_grad[...] = t_dot(joint(normed), upper_cot_ref[...]).astype(BF)
    down_grad[...] = t_dot(active_ref[...], joint(cots)).astype(BF)
    for slot, out in enumerate(outs):
        rows = pl.ds(pl.multiple_of(place_ref[1 + slot] * each, 32), each)
        out[pl.ds(0, each), :] = up_grad[rows, :]
        out[pl.ds(each, each), :] = down_grad[rows, :]


def feed_sum(place, active, upper_cot, normed, cots):
    width, inner = cots[0].shape[1], active.shape[1]
    outs = [((inner // 4, width), BF)] * 8
    scratch = [((width, inner), BF), ((inner, width), BF)]
    return call(feed_sum_kernel, "feed_sum", outs, scratch, place, active, upper_cot, *normed, *cots)


def store_kernel(fsdp, *refs):
    qkv_out, out_out, up_out, down_out = refs[6:]
    for layer in range(LAYERS):
        columns_ref, rows_ref, fed_ref = refs[3 * layer : 3 * layer + 3]
        out_out[layer] = rows_ref[...].astype(F32)
        down_out[layer] = fed_ref[pl.ds(fed_ref.shape[0] - down_out.shape[1], down_out.shape[1]), :]
        seq = columns_ref.shape[0]
        inner, group = up_out.shape[2] // seq, qkv_out.shape[2] // (3 * seq)
        for quarter in range(seq):
            values = columns_ref[quarter].astype(F32)
            each = inner // fsdp
            for part in range(fsdp):
                at = (part * seq + quarter) * each
                up_out[layer, :, pl.ds(at, each)] = values[:, part * each : part * each + each]
            for part in range(3):
                at = (part * seq + quarter) * group
                start = inner + part * group
                qkv_out[layer, :, pl.ds(at, group)] = values[:, start : start + group]


def store(sent_0, sent_1, group, seq, fsdp):
    piece, width = sent_0[1].shape
    inner = sent_0[0].shape[2] - 3 * group
    shapes = [(piece, 3 * group * seq), (piece, width), (piece, inner * seq), (inner * seq // (fsdp * seq), width)]
    outs = [((LAYERS,) + shape, F32) for shape in shapes]
    args = sent_0 + sent_1
    return pl.pallas_call(
        functools.partial(store_kernel, fsdp),
        out_shape=tuple(jax.ShapeDtypeStruct(shape, dtype) for shape, dtype in outs),
        compiler_params=pltpu.CompilerParams(vmem_limit_bytes=56 << 20),
        name="store",
    )(*args)


def norm_parts(values):
    center = values - jnp.mean(values, axis=-1, keepdims=True)
    inverse = lax.rsqrt(jnp.mean(center * center, axis=-1, keepdims=True) + NORM_EPS)
    return center * inverse, inverse


def norm_back(unit, inverse, gain, cot):
    scaled = cot * gain
    inner = scaled - jnp.mean(scaled, axis=-1, keepdims=True)
    inner = inner - unit * jnp.mean(scaled * unit, axis=-1, keepdims=True)
    return inner * inverse, jnp.sum(cot * unit, axis=0), jnp.sum(cot, axis=0)


NORM_AT = 640


def norm_kernel(place_ref, *refs):
    blocks, out_ref, both = refs[:8], refs[8], refs[9]
    each = both.shape[0] // 8
    for slot, block in enumerate(blocks):
        both[pl.ds(pl.multiple_of(place_ref[1 + slot] * each, 32), each), :] = block[...].astype(F32)
    out_ref[...] = both[...].T[:8]


def norms_of(place, blocks):
    width = blocks[0].shape[1]
    part = pl.BlockSpec((width // 8, 128), lambda step: (0, NORM_AT // 128))
    return pl.pallas_call(
        norm_kernel,
        grid=(1,),
        in_specs=[pl.BlockSpec(memory_space=pltpu.SMEM)] + [part] * 8,
        out_shape=jax.ShapeDtypeStruct((8, width), F32),
        scratch_shapes=[pltpu.VMEM((width, 128), F32)],
        name="norms_of",
    )(place, *blocks)


def shards(tokens, norm_gains, norm_shifts, w_qkv, w_out, w_up, w_down, out_grad, doc_lengths):
    tok_rows, width = tokens.shape
    fsdp, seq = lax.axis_size("fsdp"), lax.axis_size("seq")
    ruled = fsdp == 8
    length = tok_rows * seq
    group = (H // seq) * HD
    piece = w_qkv.shape[1]
    inner = w_up.shape[2] // seq
    unit_rows = w_down.shape[1]
    place = lax.axis_index("seq")

    ends = jnp.cumsum(doc_lengths[0])
    starts = ends - doc_lengths[0]
    positions = lax.iota(jnp.int32, length)
    first = jnp.max(jnp.where(positions[:, None] >= starts[None, :], starts[None, :], 0), axis=1, keepdims=True)

    def column_parts(layer):
        qkv = w_qkv[layer].astype(BF).reshape(piece, 3, seq, group).transpose(2, 0, 1, 3)
        up = w_up[layer].astype(BF).reshape(piece, fsdp, seq, unit_rows).transpose(2, 0, 1, 3)
        return qkv.reshape(seq, piece, 3 * group), up.reshape(seq, piece, inner)

    def pad_cols(values, cols):
        return jnp.pad(values, [(0, 0)] * (values.ndim - 1) + [(0, cols - values.shape[-1])])

    place_ref = jnp.concatenate([place.reshape(1).astype(jnp.int32), owners()])
    norms = jnp.stack([norm_gains, norm_shifts]).astype(BF).reshape(8, piece).T
    norms = jnp.pad(norms, ((0, 0), (NORM_AT - 3 * group, width - NORM_AT - 8)))
    qkv_parts = [None, None]
    up_parts = [None, None]
    for layer in range(LAYERS):
        qkv_parts[layer], up_parts[layer] = column_parts(layer)
    early = jnp.concatenate([qkv_parts[0], jnp.broadcast_to(norms[None], (seq,) + norms.shape)], axis=2)
    early = exchange_seq(early).reshape(seq * piece, width)
    attn_low = [None, None]
    feed_low = [None, None]

    def wide_blocks(values):
        return pad_cols(values.reshape(8, -1, values.shape[-1]), width)

    def out_blocks(rows):
        return rows.reshape(2, 4, -1, width).transpose(1, 0, 2, 3).reshape(8, -1, width)

    def out_rows_of(blocks):
        return blocks.reshape(4, 2, -1, width).transpose(1, 0, 2, 3).reshape(-1, width)

    if ruled:
        out_rows = turn(w_out.astype(BF))
        early = jnp.concatenate([early, out_rows[0]])
        mark = [early]
        first_gather = Gather(early)
        first_moved = first_gather.advance()
    else:
        mark = []
        first_steps = []
    all_tokens = gather_seq(after(tokens, *mark))
    later = jnp.concatenate([up_parts[0], pad_cols(qkv_parts[1], inner), up_parts[1]], axis=1)
    later = exchange_seq(after(later, *mark))
    up_first = later[:, :piece].reshape(seq * piece, inner)
    qkv_next = later[:, piece : 2 * piece].reshape(seq * piece, inner)
    up_next = later[:, 2 * piece :].reshape(seq * piece, inner)
    if ruled:
        first_moved = first_gather.advance(*first_moved)
        low_down = w_down.astype(BF)
        feed_gather = [
            Gather(jnp.concatenate([up_first, low_down[0]])),
            Gather(jnp.concatenate([up_next, low_down[1]])),
        ]
        attn_gather = Gather(jnp.concatenate([qkv_next, out_rows[1]]))
        first_gather.advance(feed_gather[0].blocks[0], *first_moved)
        moved = feed_gather[0].advance(*first_moved)
        first_gather.advance(first_gather.sides[2])
        first_steps = feed_gather[0].advance(first_gather.blocks[3], *moved)
        attn_low[0] = first_gather.result()
    else:
        early = lax.all_gather(early, "fsdp", axis=0, tiled=True)

        def gathered(columns):
            return lax.all_gather(columns, "fsdp", axis=0, tiled=True)

        def attn_joined(columns, rows):
            rows = lax.all_gather(rows.astype(BF), BOTH, axis=0, tiled=True)
            rows = lax.dynamic_slice_in_dim(rows, place * group, group, 0)
            return jnp.concatenate([columns.reshape(8, -1, width), out_blocks(rows)], axis=1)

        attn_low = [list(attn_joined(early, w_out[0])), list(attn_joined(gathered(qkv_next), w_out[1]))]
        for layer, columns in enumerate((up_first, up_next)):
            blocks = gathered(columns), gathered(w_down[layer].astype(BF))
            feed_low[layer] = list(jnp.concatenate([wide_blocks(part) for part in blocks], axis=1))

    norm_low = norms_of(place_ref, attn_low[0]).reshape(2, LAYERS, 2, width)
    gains, shifts = norm_low[0], norm_low[1]

    plan = {}
    if ruled:
        plan = {
            ("scatter_a", 0): [feed_gather[0], attn_gather],
            ("gather_b", 0): [feed_gather[0], attn_gather],
            ("scatter_b", 0): [attn_gather, feed_gather[1]],
            ("gather_a", 1): [attn_gather, feed_gather[1]],
            ("scatter_a", 1): [feed_gather[1]],
            ("gather_b", 1): [feed_gather[1]],
        }

    def steps(what, layer):
        def work(gate):
            return sum([each.advance(gate) for each in plan.get((what, layer), [])], [])

        return work

    def beside_main(value, what, layer):
        moved = steps(what, layer)(value)
        return after(value, *moved)

    first_cot = gather_seq(after((BRANCH_SCALE * out_grad.astype(F32)).astype(BF), all_tokens[1]))
    first_steps = first_steps + first_cot[1:]

    hidden = tokens.astype(F32)
    saved = []
    for layer in range(LAYERS):
        unit_a, inverse_a = norm_parts(hidden)
        if layer == 0:
            normed_a = (norm_parts(jnp.concatenate(all_tokens).astype(F32))[0] * gains[0, 0] + shifts[0, 0]).astype(BF)
            normed_a = [after(normed_a, *first_steps)]
        else:
            normed_a = (unit_a * gains[layer, 0] + shifts[layer, 0]).astype(BF)
            normed_a = gather_seq(normed_a, steps("gather_a", layer))
        normed_a[-1] = beside_main(normed_a[-1], "normed_a", layer)
        if ruled and layer > 0:
            attn_low[layer] = attn_gather.result()
        mixed, attended, totals, sent, kept = attend(place_ref, first, attn_low[layer], normed_a, group)
        sent = beside_main(sent, "attended", layer)
        hidden = hidden + BRANCH_SCALE * scatter_seq(sent, kept, steps("scatter_a", layer))
        unit_b, inverse_b = norm_parts(hidden)
        normed_b = (unit_b * gains[layer, 1] + shifts[layer, 1]).astype(BF)
        normed_b = gather_seq(normed_b, steps("gather_b", layer))
        normed_b[-1] = beside_main(normed_b[-1], "normed_b", layer)
        if ruled:
            feed_low[layer] = feed_gather[layer].result()
        if layer < LAYERS - 1:
            sent, kept = feed(place_ref, feed_low[layer], normed_b)
            hidden = hidden + BRANCH_SCALE * scatter_seq(sent, kept, steps("scatter_b", layer))
        saved.append((unit_a, inverse_a, normed_a, mixed, attended, totals, unit_b, inverse_b, normed_b))
    last_feed = []

    cot = out_grad.astype(F32)
    norm_sums = []
    sums_of = {}
    grads_of = {}

    def start_sum(name, blocks):
        if ruled:
            sums_of[name] = Reduce(blocks)
        else:
            grads_of[name] = jnp.stack(blocks)
        return [blocks[0]]

    def step_sums(gate, *names):
        return sum([sums_of[name].advance(gate) for name in names], []) if ruled else []

    back_plan = {
        ("gather_a", 1): [("feed", 1)],
        ("scatter_a", 1): [("feed", 1)],
        ("gather_b", 0): [("feed", 1), ("attn", 1)],
        ("scatter_b", 0): [("feed", 1), ("attn", 1)],
        ("gather_a", 0): [("feed", 0), ("attn", 1)],
        ("scatter_a", 0): [("feed", 0), ("attn", 1)],
        ("after_sum", 0): [("attn", 0)],
    }
    for layer in reversed(range(LAYERS)):
        unit_a, inverse_a, normed_a, mixed, attended, totals, unit_b, inverse_b, normed_b = saved[layer]

        def sum_steps(what):
            return lambda gate: step_sums(gate, *back_plan.get((what, layer), []))

        if layer == LAYERS - 1:
            down_cot = first_cot
        else:
            down_cot = gather_seq((BRANCH_SCALE * cot).astype(BF), sum_steps("gather_b"))
        active, upper_cot, sent, kept = feed_back(place_ref, feed_low[layer], normed_b, down_cot)

        def feed_work(gate):
            moved = start_sum(("feed", layer), feed_sum(place_ref, after(active, gate), upper_cot, normed_b, down_cot))
            return moved + sum_steps("scatter_b")(gate)

        second_cot = scatter_seq(sent, kept, feed_work)
        back, gain_sum_b, shift_sum_b = norm_back(unit_b, inverse_b, gains[layer, 1], second_cot)
        cot = cot + back

        def norm_work(gate):
            if layer == LAYERS - 1:
                parts = [after(normed_b[0], gate)] + normed_b[1:]
                last_feed.extend(feed(place_ref, feed_low[layer], parts))
            return sum_steps("gather_a")(gate) + last_feed[:1]

        attn_cot = gather_seq((BRANCH_SCALE * cot).astype(BF), norm_work)
        mixed_cot, sent, kept = attend_back(place_ref, first, attn_low[layer], mixed, totals, attn_cot)
        sent = after(sent, *sum_steps("back")(mixed_cot))

        def attn_work(gate):
            joined = attend_sum(place_ref, after(mixed_cot, gate), attended, normed_a, attn_cot)
            moved = sum_steps("scatter_a")(gate) + start_sum(("attn", layer), joined)
            return moved + sum_steps("after_sum")(gate)

        normed_cot = scatter_seq(sent, kept, attn_work)
        back, gain_sum_a, shift_sum_a = norm_back(unit_a, inverse_a, gains[layer, 0], normed_cot)
        cot = cot + back
        norm_sums.append(jnp.concatenate([gain_sum_a, gain_sum_b, shift_sum_a, shift_sum_b]))

    sent, kept = last_feed
    sums = jnp.concatenate(norm_sums[::-1])
    column_back = {}
    row_back = {}

    def send_home(layer, *gates):
        attn, fed = sums_of["attn", layer].total, sums_of["feed", layer].total
        columns = jnp.concatenate([fed[: seq * piece], attn[: seq * piece, : 3 * group]], axis=1).astype(BF)
        rows = after(attn[seq * piece :].astype(BF), *gates)
        columns = exchange_seq(after(columns, *gates).reshape(seq, piece, -1))
        return columns, turn(rows), fed

    def take(layer):
        def summed(blocks):
            return lax.psum_scatter(blocks, "fsdp", scatter_dimension=0, tiled=True).astype(F32)

        joined = grads_of["attn", layer]
        column_back["qkv", layer] = summed(joined[:, : width // 8, : 3 * group].reshape(width, 3 * group))
        rows = out_rows_of(joined[:, width // 8 :])
        spread = jnp.zeros((seq,) + rows.shape, BF)
        spread = lax.dynamic_update_index_in_dim(spread, rows, place, 0).reshape(-1, width)
        row_back["out", layer] = lax.psum_scatter(spread, BOTH, scatter_dimension=0, tiled=True).astype(F32)
        joined = grads_of["feed", layer]
        column_back["up", layer] = summed(joined[:, : width // 8].reshape(width, inner))
        row_back["down", layer] = summed(joined[:, width // 8 :].reshape(inner, width))

    def home(layer):
        both = jnp.concatenate([column_back["up", layer], column_back["qkv", layer]], axis=1).astype(BF)
        both = exchange_seq(both.reshape(seq, piece, -1)).astype(F32)
        qkv = both[:, :, inner:].reshape(seq, piece, 3, group).transpose(1, 2, 0, 3).reshape(piece, -1)
        up = both[:, :, :inner].reshape(seq, piece, fsdp, unit_rows).transpose(1, 2, 0, 3)
        return up.reshape(piece, -1), qkv

    if ruled:
        mark = sums_of["attn", 0].advance() + sums_of["feed", 0].advance()
        near = swap_seq(after(sent, cot), 1)
        sums = after(sums + swap_seq(sums, 1), *mark, near)
        half = kept.astype(F32) + near.astype(F32)
        mark = step_sums(sums, ("attn", 0), ("feed", 0))
        got = swap_seq(after(half[1].astype(BF), sums), 2)
        sums = after(sums + swap_seq(sums, 2), *mark, got)
        mark = step_sums(sums, ("attn", 0))
        sums = after(sums + lax.ppermute(sums, "fsdp", [(f, f ^ 1) for f in range(8)]), *mark)
        outputs = hidden + BRANCH_SCALE * (half[0] + got.astype(F32))
        sent_1 = send_home(1, sums)
        sums = sums + lax.ppermute(sums, "fsdp", [(f, f ^ 2) for f in range(8)])
        sent_0 = send_home(0)
        sums = after(sums, *sent_0[:2], *sent_1[:2])
        sums = sums + lax.ppermute(sums, "fsdp", [(f, f ^ 4) for f in range(8)])
        weight_grads = store(sent_0, sent_1, group, seq, fsdp)
    else:
        take(0)
        take(1)
        outputs = hidden + BRANCH_SCALE * scatter_seq(sent, kept)
        home_0, home_1 = home(0), home(1)
        sums = lax.psum(sums, BOTH)
        up_grads, qkv_grads = zip(home_0, home_1)
        out_grads = [row_back["out", layer] for layer in range(LAYERS)]
        down_grads = [row_back["down", layer] for layer in range(LAYERS)]
        weight_grads = [jnp.stack(grads) for grads in (qkv_grads, out_grads, up_grads, down_grads)]
    whose = lax.axis_index("fsdp") * seq + place
    sums = lax.dynamic_slice_in_dim(sums.reshape(-1, width), whose * piece, piece, 1).reshape(LAYERS, 4, piece)
    return (
        outputs.astype(BF),
        cot.astype(BF),
        sums[:, :2],
        sums[:, 2],
        sums[:, 3],
        *weight_grads,
    )


def solution(mesh):
    rows = P(BOTH, None)
    thirds = P(None, None, BOTH)
    middle = P(None, BOTH, None)
    return jax.shard_map(
        shards,
        mesh=mesh,
        in_specs=(rows, thirds, thirds, middle, middle, middle, middle, rows, P("fsdp", None)),
        out_specs=(rows, rows, thirds, P(None, BOTH), P(None, BOTH), middle, middle, middle, middle),
        check_vma=False,
    )
```
